512 devices in a mesh: seq: 128 (over y, z, core), ch: 4 (over x).
Axes of the slice: x: 4, y: 8, z: 8, core: 2. Of those that a mesh axis runs over, the one named last changes fastest.
Arguments:
- inputs: bfloat16 [1024, 16384], P('ch', 'seq'), may hold values from -6 to 6
- out_grad: bfloat16 [1024, 16384], P('ch', 'seq'), may hold values from -6 to 6
- readout: float32 [2, 1024, 64], P(None, 'ch'), may hold values from -4 to 4
- log_step: float32 [1024], P('ch'), may hold values from -10.5 to -3
- decay_log: float32 [64], replicated, may hold values from -1.4 to 0
- rotation: float32 [64], replicated, may hold values from 0 to 200
Outputs:
- kernel_grad: float32 [1024, 16384], P('ch', 'seq')
- readout_grad: float32 [2, 1024, 64], P(None, 'ch')
- step_grad: float32 [1024], P('ch')
- state_grad: float32 [2, 64], replicated
The draws below stay inside these ranges and needn't reach their ends.
All inputs are finite; a program needn't handle non-finite values.
Results may differ from the reference program's by a relative error of at most 0.0005.
Values may be sent and summed in bfloat16 or wider, within the bound.
A program may use at most 64 MiB of HBM per device.

```python
import math
import jax
import jax.numpy as jnp
from jax import lax

CHANNELS = 1024
STATES = 64
TOK_DEV = 128
SEQ = 16384
N_SEQ = 128


def steps_of(rng, dims, cuts, low, top_value):
    level, own = 1.0, jax.random.fold_in(rng, 6)
    for dim, parts in cuts:
        draws = jnp.exp(jax.random.uniform(jax.random.fold_in(own, dim), (parts,), jnp.float32, low / len(cuts), top_value / len(cuts)))
        level = level * jnp.repeat(draws, dims[dim] // parts).reshape([-1 if axis == dim else 1 for axis in range(len(dims))])
    return level


def scatter_about(rng, extent, scale, most, split=(), held_as=jnp.bfloat16):
    gain = steps_of(rng, extent, split, -0.22, 0.18) if split else 1.0
    result = jax.random.normal(rng, extent, jnp.float32) * scale * gain
    return jnp.minimum(jnp.maximum(result, -most), most).astype(held_as)


def setup_inputs(seed: int = 0) -> dict:
    keys = jax.random.split(jax.random.key(seed), 7)
    return {
        "inputs": scatter_about(keys[0], (CHANNELS, SEQ), 1.0, 6.0, ((0, 4), (1, 128))),
        "out_grad": scatter_about(keys[1], (CHANNELS, SEQ), 1.0, 6.0, ((0, 4), (1, 128))),
        "readout": scatter_about(keys[2], (2, CHANNELS, STATES), 1.0, 4.0, ((1, 4),), jnp.float32),
        "log_step": jnp.clip(-10.5 + 7.5 * jax.random.uniform(keys[3], (CHANNELS,), jnp.float32) ** steps_of(keys[3], (CHANNELS,), ((0, 4),), -0.2, 0.2), -10.5, -3.0),
        "decay_log": jnp.clip(jax.random.uniform(keys[4], (STATES,), jnp.float32, -1.4, 0.0), -1.4, 0.0),
        "rotation": jnp.clip(jax.random.uniform(keys[5], (STATES,), jnp.float32, 0.0, 200.0), 0.0, 200.0),
    }


precise = lax.Precision.HIGHEST

def discretize(readout, log_step, decay_log, rotation):
    step_size = jnp.exp(log_step)[:, None]
    pole_real = -jnp.exp(decay_log)[None, :]
    pole_imag = rotation[None, :]
    rate_real = step_size * pole_real
    rate_imag = step_size * pole_imag
    lift_real = jnp.expm1(rate_real) * jnp.cos(rate_imag) - 2.0 * jnp.sin(0.5 * rate_imag) ** 2
    lift_imag = jnp.exp(rate_real) * jnp.sin(rate_imag)
    pole_norm = pole_real * pole_real + pole_imag * pole_imag
    ratio_real = (lift_real * pole_real + lift_imag * pole_imag) / pole_norm
    ratio_imag = (lift_imag * pole_real - lift_real * pole_imag) / pole_norm
    coef_real = readout[0] * ratio_real - readout[1] * ratio_imag
    coef_imag = readout[0] * ratio_imag + readout[1] * ratio_real
    return (coef_real, coef_imag, rate_real, rate_imag)

def parameter_grads(primal, backward, totals):
    coef_real, coef_imag = (primal[0], primal[1])
    cotangents = (2.0 * totals[0], -2.0 * totals[1], 2.0 * (coef_real * totals[2] - coef_imag * totals[3]), -2.0 * (coef_real * totals[3] + coef_imag * totals[2]))
    return backward(cotangents)

def shifted_totals(raw_sums, rate_real, rate_imag, block_start, norm_scale):
    decays = jnp.exp(rate_real * block_start)
    phases = rate_imag * block_start
    base_real = decays * jnp.cos(phases)
    base_imag = decays * jnp.sin(phases)
    near_real = block_start * raw_sums[0] + raw_sums[2]
    near_imag = block_start * raw_sums[1] + raw_sums[3]
    return jnp.stack([norm_scale * (base_real * raw_sums[0] - base_imag * raw_sums[1]), norm_scale * (base_real * raw_sums[1] + base_imag * raw_sums[0]), norm_scale * (base_real * near_real - base_imag * near_imag), norm_scale * (base_real * near_imag + base_imag * near_real)])

def reference(inputs, out_grad, readout, log_step, decay_log, rotation):
    norm_scale = 1.0 / math.sqrt(SEQ)
    group_size = math.gcd(CHANNELS, 64)
    group_count = CHANNELS // group_size

    def correlate(pieces):
        padded_in = jnp.pad(pieces[0].astype(jnp.float32), ((0, 0), (0, SEQ)))
        padded_out = jnp.pad(pieces[1].astype(jnp.float32), ((0, 0), (0, SEQ)))
        spectrum = jnp.fft.fft(padded_out, axis=-1) * jnp.conj(jnp.fft.fft(padded_in, axis=-1))
        lagged = jnp.real(jnp.fft.ifft(spectrum, axis=-1))[:, :SEQ]
        return (lagged * norm_scale).astype(jnp.float32)
    kernel_grad = lax.map(correlate, (inputs.reshape(group_count, group_size, SEQ), out_grad.reshape(group_count, group_size, SEQ))).reshape(CHANNELS, SEQ)
    primal, backward = jax.vjp(discretize, readout, log_step, decay_log, rotation)
    offsets = jnp.arange(TOK_DEV, dtype=jnp.int32).astype(jnp.float32)
    starts = (jnp.arange(N_SEQ, dtype=jnp.int32) * TOK_DEV).astype(jnp.float32)

    def block_totals(pieces):
        lag_rows, real_rate, imag_rate = pieces
        blocks = lag_rows.reshape(group_size, N_SEQ, TOK_DEV)
        decays = jnp.exp(real_rate[:, :, None] * offsets)
        phases = imag_rate[:, :, None] * offsets
        power_real = decays * jnp.cos(phases)
        power_imag = decays * jnp.sin(phases)
        weighted = blocks * offsets
        raw_sums = jnp.stack([jnp.einsum('gbj,gnj->gnb', blocks, power_real, precision=precise), jnp.einsum('gbj,gnj->gnb', blocks, power_imag, precision=precise), jnp.einsum('gbj,gnj->gnb', weighted, power_real, precision=precise), jnp.einsum('gbj,gnj->gnb', weighted, power_imag, precision=precise)])
        totals = shifted_totals(raw_sums, real_rate[:, :, None], imag_rate[:, :, None], starts, norm_scale)
        return lax.optimization_barrier(jnp.sum(totals, axis=-1))
    totals = lax.map(block_totals, (kernel_grad.reshape(group_count, group_size, SEQ), primal[2].reshape(group_count, group_size, STATES), primal[3].reshape(group_count, group_size, STATES)))
    totals = jnp.transpose(totals, (1, 0, 2, 3)).reshape(4, CHANNELS, STATES)
    readout_grad, step_grad, decay_grad, rotation_grad = parameter_grads(primal, backward, totals)
    return (kernel_grad, readout_grad, step_grad, jnp.stack([decay_grad, rotation_grad]))
```

```python
import functools
import math

import jax
import jax.numpy as jnp
import numpy as np
from jax import lax
from jax.experimental import pallas as pl
from jax.experimental.pallas import tpu as pltpu
from jax.sharding import PartitionSpec as P

MESH = pl.DeviceIdType.MESH
RINGS = (8, 8, 2)
OWNERS = 128
WIDTH = 128
LENGTH = OWNERS * WIDTH
STATES = 64


def split_table(table):
    whole = jnp.asarray(np.asarray(table, np.float32))
    high = np.asarray(table, np.float32).astype(jnp.bfloat16)
    low = (np.asarray(table, np.float64) - high.astype(np.float64)).astype(jnp.bfloat16)
    del whole
    return np.stack([high, low])


def transform_tables():
    index = np.arange(WIDTH, dtype=np.float64)
    quarter = index + 0.25
    enter = 2.0 * np.pi * np.outer(quarter, index) / WIDTH
    spread = np.zeros((2, 2, WIDTH, OWNERS, 2))
    for channel in range(2):
        spread[0, channel, :, :, channel] = np.cos(enter)
        spread[1, channel, :, :, channel] = -np.sin(enter)
    first = spread.reshape(4 * WIDTH, 2 * OWNERS)
    turn = 2.0 * np.pi * np.outer(quarter, index) / LENGTH
    turns = np.stack([np.cos(turn), np.sin(turn)]).astype(np.float32)
    plain = 2.0 * np.pi * np.outer(index, index) / WIDTH
    cosine, sine = np.cos(plain), np.sin(plain)
    second = np.block([[cosine, -sine], [sine, cosine]])
    third = np.block([[cosine, sine], [-sine, cosine]])
    scale = 1.0 / (LENGTH * math.sqrt(LENGTH))
    leave = enter.T
    fourth = np.concatenate([np.cos(leave), -np.sin(leave)], axis=1) * scale
    return (
        split_table(first),
        turns,
        split_table(second),
        split_table(third),
        split_table(fourth),
    )


def dot(left, right):
    return jnp.dot(left, right, preferred_element_type=jnp.float32)


def halves(value):
    high = value.astype(jnp.bfloat16)
    return high, (value - high.astype(jnp.float32)).astype(jnp.bfloat16)


def dot_pair(left, right):
    return dot(left[0], right[0]) + (dot(left[0], right[1]) + dot(left[1], right[0]))


def sine_cosine(angle):
    turns = jnp.floor(angle * (2.0 / math.pi) + 0.5)
    rest = angle - turns * 1.5625
    rest = rest - turns * 0.0081787109375
    rest = rest - turns * 0.000116348266601562
    rest = rest - turns * 1.26759079665e-06
    square = rest * rest
    sine = rest + rest * square * (
        -1.6666667e-1 + square * (8.3333310e-3 + square * (-1.9840874e-4 + square * 2.7525562e-6))
    )
    cosine = (
        1.0
        - 0.5 * square
        + square
        * square
        * (4.16666667e-2 + square * (-1.38888889e-3 + square * (2.48015873e-5 - square * 2.7557319e-7)))
    )
    quadrant = turns - 4.0 * jnp.floor(turns * 0.25)
    odd = (quadrant == 1.0) | (quadrant == 3.0)
    sine_out = jnp.where(odd, cosine, sine)
    cosine_out = jnp.where(odd, sine, cosine)
    sine_out = jnp.where(quadrant >= 2.0, -sine_out, sine_out)
    cosine_out = jnp.where((quadrant == 1.0) | (quadrant == 2.0), -cosine_out, cosine_out)
    return sine_out, cosine_out


def exp_minus_one(value):
    series = 1.0 + value * (1.0 / 9.0)
    for count in (8.0, 7.0, 6.0, 5.0, 4.0, 3.0, 2.0):
        series = 1.0 + value * (1.0 / count) * series
    return jnp.where(jnp.abs(value) < 0.5, value * series, jnp.exp(value) - 1.0)


def multiply(left, right):
    return (left[0] * right[0] - left[1] * right[1], left[0] * right[1] + left[1] * right[0])


def conjugate(value):
    return (value[0], -value[1])


def primal_rows(step, decay, turn, readout):
    pole = (-jnp.exp(decay), turn)
    rate = (step * pole[0], step * pole[1])
    sine, cosine = sine_cosine(rate[1])
    half_sine, _ = sine_cosine(0.5 * rate[1])
    growth = jnp.exp(rate[0])
    lift = (
        exp_minus_one(rate[0]) * cosine - 2.0 * half_sine * half_sine,
        growth * sine,
    )
    norm = pole[0] * pole[0] + pole[1] * pole[1]
    inverse = (pole[0] / norm, -pole[1] / norm)
    ratio = multiply(lift, inverse)
    coef = multiply(readout, ratio)
    power = (growth * cosine, growth * sine)
    return dict(
        step=step, pole=pole, rate=rate, inverse=inverse, ratio=ratio, coef=coef, power=power
    )


def power_table(rate, positions):
    decays = jnp.exp(rate[0] * positions)
    sine, cosine = sine_cosine(rate[1] * positions)
    return decays * cosine, decays * sine


def correlate(signals, first, turns, second, third, fourth):
    spread = dot(first[0], signals) + dot(first[1], signals)
    turn_cos, turn_sin = turns[0], turns[1]
    blocks = []
    for channel in range(2):
        for signal in range(2):
            columns = slice(signal * WIDTH, (signal + 1) * WIDTH)
            real = spread[channel * WIDTH : (channel + 1) * WIDTH, columns]
            imag = spread[(2 + channel) * WIDTH : (3 + channel) * WIDTH, columns]
            blocks.append(
                jnp.concatenate(
                    [real * turn_cos + imag * turn_sin, imag * turn_cos - real * turn_sin], axis=1
                )
            )
    spectrum = dot_pair(halves(jnp.concatenate(blocks, axis=0)), second)
    products = []
    for channel in range(2):
        entry = spectrum[2 * channel * WIDTH : (2 * channel + 1) * WIDTH]
        exit_ = spectrum[(2 * channel + 1) * WIDTH : (2 * channel + 2) * WIDTH]
        in_real, in_imag = entry[:, :WIDTH], entry[:, WIDTH:]
        out_real, out_imag = exit_[:, :WIDTH], exit_[:, WIDTH:]
        products.append(
            jnp.concatenate(
                [
                    out_real * in_real + out_imag * in_imag,
                    out_imag * in_real - out_real * in_imag,
                ],
                axis=1,
            )
        )
    back = dot_pair(halves(jnp.concatenate(products, axis=0)), third)
    columns = []
    for channel in range(2):
        real = back[channel * WIDTH : (channel + 1) * WIDTH, :WIDTH]
        imag = back[channel * WIDTH : (channel + 1) * WIDTH, WIDTH:]
        columns.append(
            jnp.concatenate(
                [real * turn_cos - imag * turn_sin, real * turn_sin + imag * turn_cos], axis=0
            )
        )
    return dot_pair((fourth[0], fourth[1]), halves(jnp.concatenate(columns, axis=1)))


def sum_rows(value):
    return jnp.sum(value, axis=0, keepdims=True)


def power_sums(lags, near, base, starts, offsets, norm_scale):
    stacked = jnp.concatenate([lags[:, :WIDTH], lags[:, WIDTH:]], axis=0)
    tables = jnp.concatenate(
        [near[0], near[1], offsets * near[0], offsets * near[1]], axis=1
    )
    raw = dot_pair(halves(stacked), halves(tables))
    lane = lax.broadcasted_iota(jnp.int32, (OWNERS, WIDTH), 1)
    picked = [
        jnp.where(
            lane < STATES,
            raw[:OWNERS, part * WIDTH : (part + 1) * WIDTH],
            raw[OWNERS:, part * WIDTH : (part + 1) * WIDTH],
        )
        for part in range(4)
    ]
    plain = (picked[0], picked[1])
    lagged = (starts * picked[0] + picked[2], starts * picked[1] + picked[3])
    powers = multiply(base, plain)
    lag_powers = multiply(base, lagged)
    return (
        (norm_scale * sum_rows(powers[0]), norm_scale * sum_rows(powers[1])),
        (norm_scale * sum_rows(lag_powers[0]), norm_scale * sum_rows(lag_powers[1])),
    )


def parameter_rows(primal, readout, powers, lag_powers):
    coef_grad = (2.0 * powers[0], -2.0 * powers[1])
    readout_grad = multiply(conjugate(primal["ratio"]), coef_grad)
    ratio_grad = multiply(conjugate(readout), coef_grad)
    shifted = multiply(primal["coef"], lag_powers)
    lift_grad = multiply(conjugate(primal["inverse"]), ratio_grad)
    through = multiply(conjugate(primal["power"]), lift_grad)
    rate_grad = (2.0 * shifted[0] + through[0], -2.0 * shifted[1] + through[1])
    direct = multiply(conjugate(primal["ratio"]), lift_grad)
    step, pole = primal["step"], primal["pole"]
    pole_grad = (step * rate_grad[0] - direct[0], step * rate_grad[1] - direct[1])
    step_terms = step * (rate_grad[0] * pole[0] + rate_grad[1] * pole[1])
    return readout_grad, step_terms, (pole_grad[0] * pole[0], pole_grad[1])


def offset_of(place, ring):
    return ring // 2 + (1 - 2 * (place % 2)) * ((place + 1) // 2)


def peer_of(me, count):
    y, z, core = me // 16, (me // 2) % 8, me % 2
    to_y = (y + offset_of(count // 16, 8)) % 8
    to_z = (z + offset_of((count // 2) % 8, 8)) % 8
    to_core = (core + 1 - count % 2) % 2
    return to_y * 16 + to_z * 2 + to_core


def per_peer(me, action):
    def step(count, carry):
        action(peer_of(me, count))
        return carry

    lax.fori_loop(0, OWNERS - 1, step, 0)


def kernel(
    norm_scale,
    inputs_ref,
    grads_ref,
    readout_ref,
    log_step_ref,
    states_ref,
    first_ref,
    turns_ref,
    second_ref,
    third_ref,
    fourth_ref,
    lags_out,
    params_out,
    shared_out,
    outgoing,
    arrived,
    lag_rows,
    param_rows,
    state_rows,
    state_sums,
    state_in,
    first,
    turns,
    second,
    third,
    fourth,
    stage_sem,
    table_sem,
    own_sem,
    send_sem,
    signal_sem,
    lag_sem,
    param_sem,
    state_sem,
    cross_sem,
    cross_send_sem,
):
    me = lax.axis_index("seq")
    row = lax.axis_index("ch")
    stages = [
        pltpu.make_async_copy(inputs_ref, outgoing.at[0], stage_sem.at[0]),
        pltpu.make_async_copy(grads_ref, outgoing.at[1], stage_sem.at[1]),
    ]
    loads = [
        pltpu.make_async_copy(source, target, table_sem.at[place])
        for place, (source, target) in enumerate(
            (
                (first_ref, first),
                (turns_ref, turns),
                (second_ref, second),
                (third_ref, third),
                (fourth_ref, fourth),
            )
        )
    ]
    for copy in stages:
        copy.start()
    for copy in loads:
        copy.start()
    barrier = pltpu.get_barrier_semaphore()

    def greet(peer):
        pl.semaphore_signal(barrier, inc=1, device_id={"seq": peer}, device_id_type=MESH)

    per_peer(me, greet)
    for step in range(1, 4):
        pl.semaphore_signal(
            barrier, inc=1, device_id={"ch": (row + step) % 4}, device_id_type=MESH
        )
    for copy in stages:
        copy.wait()
    pl.semaphore_wait(barrier, OWNERS - 1 + 3)

    def exchange(source, target, send, receive):
        def action(peer):
            pltpu.make_async_remote_copy(
                src_ref=source(peer),
                dst_ref=target,
                send_sem=send,
                recv_sem=receive,
                device_id={"seq": peer},
                device_id_type=MESH,
            ).start()

        per_peer(me, action)

    own = pltpu.make_async_copy(outgoing.at[:, me], arrived.at[:, me], own_sem.at[0])
    own.start()
    exchange(lambda peer: outgoing.at[:, peer], arrived.at[:, me], send_sem.at[0], signal_sem)

    lane_row = lax.broadcasted_iota(jnp.int32, (1, WIDTH), 1)
    step_row = jnp.exp(
        jnp.where(lane_row < STATES, log_step_ref[2 * me], log_step_ref[2 * me + 1])
    )
    decay_row = states_ref[0:1, :]
    turn_row = states_ref[1:2, :]
    readout = (readout_ref[0, pl.ds(me, 1), :], readout_ref[1, pl.ds(me, 1), :])
    primal = primal_rows(step_row, decay_row, turn_row, readout)
    offsets = lax.broadcasted_iota(jnp.int32, (WIDTH, WIDTH), 0).astype(jnp.float32)
    starts = offsets * float(WIDTH)
    near = power_table(primal["rate"], offsets)
    base = power_table(primal["rate"], starts)
    for copy in loads:
        copy.wait()

    own.wait()
    rest = arrived.at[:, pl.ds(0, OWNERS - 1)]
    pltpu.make_async_copy(rest, rest, signal_sem).wait()
    signals = jnp.concatenate(
        [arrived.reshape(2, 2 * OWNERS, WIDTH)[0], arrived.reshape(2, 2 * OWNERS, WIDTH)[1]],
        axis=1,
    )
    lags = correlate(signals, first, turns, second, third, fourth)
    lag_rows[:, 0, :] = lags[:, :WIDTH]
    lag_rows[:, 1, :] = lags[:, WIDTH:]
    own_lags = pltpu.make_async_copy(lag_rows.at[me], lags_out.at[me], own_sem.at[1])
    own_lags.start()
    exchange(lambda peer: lag_rows.at[peer], lags_out.at[me], send_sem.at[1], lag_sem)

    powers, lag_powers = power_sums(lags, near, base, starts, offsets, norm_scale)
    readout_grad, step_terms, state_grad = parameter_rows(primal, readout, powers, lag_powers)
    step_grad = jnp.where(
        lane_row < STATES,
        jnp.sum(jnp.where(lane_row < STATES, step_terms, 0.0), axis=1, keepdims=True),
        jnp.sum(jnp.where(lane_row < STATES, 0.0, step_terms), axis=1, keepdims=True),
    )
    param_rows[0:1, :] = readout_grad[0]
    param_rows[1:2, :] = readout_grad[1]
    param_rows[2:3, :] = step_grad
    param_rows[3:4, :] = jnp.zeros_like(step_grad)
    own_params = pltpu.make_async_copy(param_rows, params_out.at[me], own_sem.at[2])
    own_params.start()
    state_rows[0:1, :] = state_grad[0]
    state_rows[1:2, :] = state_grad[1]
    crossings = [
        pltpu.make_async_remote_copy(
            src_ref=state_rows,
            dst_ref=state_in.at[step - 1],
            send_sem=cross_send_sem.at[step - 1],
            recv_sem=cross_sem.at[step - 1],
            device_id={"ch": (row + step) % 4},
            device_id_type=MESH,
        )
        for step in range(1, 4)
    ]
    for copy in crossings:
        copy.start()
    exchange(lambda peer: param_rows, params_out.at[me], send_sem.at[2], param_sem)
    for copy in crossings:
        copy.wait()
    state_sums[...] = state_rows[...] + state_in[1] + (state_in[0] + state_in[2])
    own_state = pltpu.make_async_copy(state_sums, shared_out.at[me], own_sem.at[3])
    own_state.start()
    exchange(lambda peer: state_sums, shared_out.at[me], send_sem.at[3], state_sem)

    for copy in (own_lags, own_params, own_state):
        copy.wait()
    for buffer, semaphore in (
        (lags_out, lag_sem),
        (params_out, param_sem),
        (shared_out, state_sem),
    ):
        part = buffer.at[pl.ds(0, OWNERS - 1)]
        pltpu.make_async_copy(part, part, semaphore).wait()
    pltpu.make_async_copy(rest, rest, send_sem.at[0]).wait()
    for buffer, place in ((lags_out, 1), (params_out, 2), (shared_out, 3)):
        part = buffer.at[pl.ds(0, OWNERS - 1)]
        pltpu.make_async_copy(part, part, send_sem.at[place]).wait()


def per_device(tables, inputs, out_grad, readout, log_step, decay_log, rotation):
    norm_scale = 1.0 / math.sqrt(LENGTH)
    states = jnp.stack(
        [jnp.concatenate([decay_log, decay_log]), jnp.concatenate([rotation, rotation])]
    )
    dma = pltpu.SemaphoreType.DMA
    any_space = pl.BlockSpec(memory_space=pl.ANY)
    vmem = pl.BlockSpec(memory_space=pltpu.VMEM)
    smem = pl.BlockSpec(memory_space=pltpu.SMEM)
    lags, params, shared = pl.pallas_call(
        functools.partial(kernel, norm_scale),
        out_shape=(
            jax.ShapeDtypeStruct((OWNERS, 2, WIDTH), jnp.float32),
            jax.ShapeDtypeStruct((OWNERS, 4, WIDTH), jnp.float32),
            jax.ShapeDtypeStruct((OWNERS, 2, WIDTH), jnp.float32),
        ),
        in_specs=[any_space, any_space, vmem, smem, vmem] + [any_space] * 5,
        out_specs=(vmem, vmem, vmem),
        scratch_shapes=[
            pltpu.VMEM((2, OWNERS, 2, WIDTH), jnp.bfloat16),
            pltpu.VMEM((2, OWNERS, 2, WIDTH), jnp.bfloat16),
            pltpu.VMEM((OWNERS, 2, WIDTH), jnp.float32),
            pltpu.VMEM((4, WIDTH), jnp.float32),
            pltpu.VMEM((2, WIDTH), jnp.float32),
            pltpu.VMEM((2, WIDTH), jnp.float32),
            pltpu.VMEM((3, 2, WIDTH), jnp.float32),
        ]
        + [pltpu.VMEM(table.shape, table.dtype) for table in tables]
        + [
            dma((2,)),
            dma((5,)),
            dma((4,)),
            dma((4,)),
            dma,
            dma,
            dma,
            dma,
            dma((3,)),
            dma((3,)),
        ],
        compiler_params=pltpu.CompilerParams(collective_id=0, has_side_effects=True),
        name="channel_rows",
    )(
        inputs.reshape(OWNERS, 2, WIDTH),
        out_grad.reshape(OWNERS, 2, WIDTH),
        readout.reshape(2, OWNERS, WIDTH),
        log_step,
        states,
        *[jnp.asarray(table) for table in tables],
    )
    kernel_grad = lags.reshape(2 * OWNERS, WIDTH)
    readout_grad = jnp.transpose(params[:, :2, :], (1, 0, 2)).reshape(2, 2 * OWNERS, STATES)
    step_grad = params[:, 2, :].reshape(2 * OWNERS, STATES)[:, 0]
    state = jnp.sum(shared, axis=0).reshape(2, 2, STATES)
    return kernel_grad, readout_grad, step_grad, state[:, 0] + state[:, 1]


def solution(mesh):
    tables = transform_tables()
    return jax.shard_map(
        functools.partial(per_device, tables),
        mesh=mesh,
        in_specs=(P("ch", "seq"), P("ch", "seq"), P(None, "ch", None), P("ch"), P(), P()),
        out_specs=(P("ch", "seq"), P(None, "ch", None), P("ch"), P()),
        check_vma=False,
    )
```

```python
import functools
import math

import jax
import jax.numpy as jnp
import numpy as np
from jax import lax
from jax.experimental import pallas as pl
from jax.experimental.pallas import tpu as pltpu
from jax.sharding import PartitionSpec as P

MESH = pl.DeviceIdType.MESH
OWNERS = 128
WIDTH = 128
LENGTH = OWNERS * WIDTH
STATES = 64


def split_table(table):
    high = np.asarray(table, np.float32).astype(jnp.bfloat16)
    low = (np.asarray(table, np.float64) - high.astype(np.float64)).astype(jnp.bfloat16)
    return np.stack([high, low])


def transform_tables():
    index = np.arange(WIDTH, dtype=np.float64)
    quarter = index + 0.25
    enter = 2.0 * np.pi * np.outer(quarter, index) / WIDTH
    spread = np.zeros((2, 2, WIDTH, OWNERS, 2))
    for channel in range(2):
        spread[0, channel, :, :, channel] = np.cos(enter)
        spread[1, channel, :, :, channel] = -np.sin(enter)
    first = spread.reshape(4 * WIDTH, 2 * OWNERS)
    turn = 2.0 * np.pi * np.outer(quarter, index) / LENGTH
    turns = np.stack([np.cos(turn), np.sin(turn)]).astype(np.float32)
    plain = 2.0 * np.pi * np.outer(index, index) / WIDTH
    cosine, sine = np.cos(plain), np.sin(plain)
    second = np.block([[cosine, -sine], [sine, cosine]])
    third = np.block([[cosine, sine], [-sine, cosine]])
    scale = 1.0 / (LENGTH * math.sqrt(LENGTH))
    leave = enter.T
    fourth = np.concatenate([np.cos(leave), -np.sin(leave)], axis=1) * scale
    return (
        split_table(first),
        turns,
        split_table(second),
        split_table(third),
        split_table(fourth),
    )


def dot(left, right):
    return jnp.dot(left, right, preferred_element_type=jnp.float32)


def halves(value):
    high = value.astype(jnp.bfloat16)
    return high, (value - high.astype(jnp.float32)).astype(jnp.bfloat16)


def dot_pair(left, right):
    return dot(left[0], right[0]) + (dot(left[0], right[1]) + dot(left[1], right[0]))


def sine_cosine(angle):
    turns = jnp.floor(angle * (2.0 / math.pi) + 0.5)
    rest = angle - turns * 1.5625
    rest = rest - turns * 0.0081787109375
    rest = rest - turns * 0.000116348266601562
    rest = rest - turns * 1.26759079665e-06
    square = rest * rest
    sine = rest + rest * square * (
        -1.6666667e-1 + square * (8.3333310e-3 + square * (-1.9840874e-4 + square * 2.7525562e-6))
    )
    cosine = (
        1.0
        - 0.5 * square
        + square
        * square
        * (4.16666667e-2 + square * (-1.38888889e-3 + square * (2.48015873e-5 - square * 2.7557319e-7)))
    )
    quadrant = turns - 4.0 * jnp.floor(turns * 0.25)
    odd = (quadrant == 1.0) | (quadrant == 3.0)
    sine_out = jnp.where(odd, cosine, sine)
    cosine_out = jnp.where(odd, sine, cosine)
    sine_out = jnp.where(quadrant >= 2.0, -sine_out, sine_out)
    cosine_out = jnp.where((quadrant == 1.0) | (quadrant == 2.0), -cosine_out, cosine_out)
    return sine_out, cosine_out


def exp_minus_one(value):
    series = 1.0 + value * (1.0 / 9.0)
    for count in (8.0, 7.0, 6.0, 5.0, 4.0, 3.0, 2.0):
        series = 1.0 + value * (1.0 / count) * series
    return jnp.where(jnp.abs(value) < 0.5, value * series, jnp.exp(value) - 1.0)


def multiply(left, right):
    return (left[0] * right[0] - left[1] * right[1], left[0] * right[1] + left[1] * right[0])


def conjugate(value):
    return (value[0], -value[1])


def primal_rows(step, decay, turn, readout):
    pole = (-jnp.exp(decay), turn)
    rate = (step * pole[0], step * pole[1])
    sine, cosine = sine_cosine(rate[1])
    half_sine, _ = sine_cosine(0.5 * rate[1])
    growth = jnp.exp(rate[0])
    lift = (
        exp_minus_one(rate[0]) * cosine - 2.0 * half_sine * half_sine,
        growth * sine,
    )
    norm = pole[0] * pole[0] + pole[1] * pole[1]
    inverse = (pole[0] / norm, -pole[1] / norm)
    ratio = multiply(lift, inverse)
    coef = multiply(readout, ratio)
    power = (growth * cosine, growth * sine)
    return dict(
        step=step, pole=pole, rate=rate, inverse=inverse, ratio=ratio, coef=coef, power=power
    )


def power_table(rate, positions):
    decays = jnp.exp(rate[0] * positions)
    sine, cosine = sine_cosine(rate[1] * positions)
    return decays * cosine, decays * sine


def correlate(signals, first, turns, second, third, fourth):
    spread = dot(first[0], signals) + dot(first[1], signals)
    turn_cos, turn_sin = turns[0], turns[1]
    blocks = []
    for channel in range(2):
        for signal in range(2):
            columns = slice(signal * WIDTH, (signal + 1) * WIDTH)
            real = spread[channel * WIDTH : (channel + 1) * WIDTH, columns]
            imag = spread[(2 + channel) * WIDTH : (3 + channel) * WIDTH, columns]
            blocks.append(
                jnp.concatenate(
                    [real * turn_cos + imag * turn_sin, imag * turn_cos - real * turn_sin], axis=1
                )
            )
    spectrum = dot_pair(halves(jnp.concatenate(blocks, axis=0)), second)
    products = []
    for channel in range(2):
        entry = spectrum[2 * channel * WIDTH : (2 * channel + 1) * WIDTH]
        exit_ = spectrum[(2 * channel + 1) * WIDTH : (2 * channel + 2) * WIDTH]
        in_real, in_imag = entry[:, :WIDTH], entry[:, WIDTH:]
        out_real, out_imag = exit_[:, :WIDTH], exit_[:, WIDTH:]
        products.append(
            jnp.concatenate(
                [
                    out_real * in_real + out_imag * in_imag,
                    out_imag * in_real - out_real * in_imag,
                ],
                axis=1,
            )
        )
    back = dot_pair(halves(jnp.concatenate(products, axis=0)), third)
    columns = []
    for channel in range(2):
        real = back[channel * WIDTH : (channel + 1) * WIDTH, :WIDTH]
        imag = back[channel * WIDTH : (channel + 1) * WIDTH, WIDTH:]
        columns.append(
            jnp.concatenate(
                [real * turn_cos - imag * turn_sin, real * turn_sin + imag * turn_cos], axis=0
            )
        )
    return dot_pair((fourth[0], fourth[1]), halves(jnp.concatenate(columns, axis=1)))


def sum_rows(value):
    return jnp.sum(value, axis=0, keepdims=True)


def power_sums(lags, tables, base, starts, norm_scale):
    stacked = jnp.concatenate([lags[:, :WIDTH], lags[:, WIDTH:]], axis=0)
    raw = dot_pair(halves(stacked), tables)
    lane = lax.broadcasted_iota(jnp.int32, (OWNERS, WIDTH), 1)
    picked = [
        jnp.where(
            lane < STATES,
            raw[:OWNERS, part * WIDTH : (part + 1) * WIDTH],
            raw[OWNERS:, part * WIDTH : (part + 1) * WIDTH],
        )
        for part in range(4)
    ]
    plain = (picked[0], picked[1])
    lagged = (starts * picked[0] + picked[2], starts * picked[1] + picked[3])
    powers = multiply(base, plain)
    lag_powers = multiply(base, lagged)
    return (
        (norm_scale * sum_rows(powers[0]), norm_scale * sum_rows(powers[1])),
        (norm_scale * sum_rows(lag_powers[0]), norm_scale * sum_rows(lag_powers[1])),
    )


def parameter_rows(primal, readout, powers, lag_powers):
    coef_grad = (2.0 * powers[0], -2.0 * powers[1])
    readout_grad = multiply(conjugate(primal["ratio"]), coef_grad)
    ratio_grad = multiply(conjugate(readout), coef_grad)
    shifted = multiply(primal["coef"], lag_powers)
    lift_grad = multiply(conjugate(primal["inverse"]), ratio_grad)
    through = multiply(conjugate(primal["power"]), lift_grad)
    rate_grad = (2.0 * shifted[0] + through[0], -2.0 * shifted[1] + through[1])
    direct = multiply(conjugate(primal["ratio"]), lift_grad)
    step, pole = primal["step"], primal["pole"]
    pole_grad = (step * rate_grad[0] - direct[0], step * rate_grad[1] - direct[1])
    step_terms = step * (rate_grad[0] * pole[0] + rate_grad[1] * pole[1])
    return readout_grad, step_terms, (pole_grad[0] * pole[0], pole_grad[1])


def offset_of(place, ring):
    return ring // 2 + (1 - 2 * (place % 2)) * ((place + 1) // 2)


def place_of(me):
    return me // 16, (me // 2) % 8, me % 2


def ring_places(place, ring):
    return [(place + offset_of(count, ring)) % ring for count in range(ring)]


def per_peer(me, action):
    y, z, core = place_of(me)
    to_y = [16 * other for other in ring_places(y, 8)]
    to_z = [2 * other for other in ring_places(z, 8)]
    to_core = [1 - core, core]
    peers = [at_y + at_z + at_core for at_y in to_y for at_z in to_z for at_core in to_core]
    for peer in peers[:-1]:
        action(peer)


def kernel(
    norm_scale,
    inputs_ref,
    grads_ref,
    readout_ref,
    log_step_ref,
    decay_ref,
    rotation_ref,
    first_ref,
    turns_ref,
    second_ref,
    third_ref,
    fourth_ref,
    lags_out,
    readout_out,
    sums_out,
    outgoing,
    arrived,
    lag_rows,
    readout_rows,
    readout_turned,
    cross_rows,
    cross_in,
    line_rows,
    line_in,
    column_rows,
    column_in,
    first,
    turns,
    second,
    third,
    fourth,
    stage_sem,
    table_sem,
    own_sem,
    send_sem,
    signal_sem,
    lag_sem,
    readout_sem,
    cross_sem,
    line_sem,
    column_sem,
):
    me = lax.axis_index("seq")
    row = lax.axis_index("ch")
    y, z, core = place_of(me)
    barrier = pltpu.get_barrier_semaphore()

    def greet(peer):
        pl.semaphore_signal(barrier, inc=1, device_id={"seq": peer}, device_id_type=MESH)

    per_peer(me, greet)
    rows_across = [(row + step) % 4 for step in range(1, 4)]
    for other in rows_across:
        pl.semaphore_signal(barrier, inc=1, device_id={"ch": other}, device_id_type=MESH)
    stages = [
        pltpu.make_async_copy(inputs_ref, outgoing.at[0], stage_sem.at[0]),
        pltpu.make_async_copy(grads_ref, outgoing.at[1], stage_sem.at[1]),
    ]
    loads = [
        pltpu.make_async_copy(source, target, table_sem.at[place])
        for place, (source, target) in enumerate(
            (
                (first_ref, first),
                (turns_ref, turns),
                (second_ref, second),
                (third_ref, third),
                (fourth_ref, fourth),
            )
        )
    ]
    for copy in stages:
        copy.start()
    for copy in loads:
        copy.start()
    for copy in stages:
        copy.wait()
    pl.semaphore_wait(barrier, OWNERS - 1 + 3)

    def send(source, target, sent, received, device):
        pltpu.make_async_remote_copy(
            src_ref=source,
            dst_ref=target,
            send_sem=sent,
            recv_sem=received,
            device_id=device,
            device_id_type=MESH,
        ).start()

    own = pltpu.make_async_copy(outgoing.at[:, me], arrived.at[:, me], own_sem.at[0])
    own.start()
    per_peer(
        me,
        lambda peer: send(
            outgoing.at[:, peer], arrived.at[:, me], send_sem.at[0], signal_sem, {"seq": peer}
        ),
    )

    lane_row = lax.broadcasted_iota(jnp.int32, (1, WIDTH), 1)
    left = lane_row < STATES
    step_row = jnp.exp(jnp.where(left, log_step_ref[2 * me], log_step_ref[2 * me + 1]))
    decay_row = jnp.concatenate([decay_ref[...], decay_ref[...]], axis=1)
    turn_row = jnp.concatenate([rotation_ref[...], rotation_ref[...]], axis=1)
    readout_turned[...] = jnp.transpose(
        jnp.concatenate([readout_ref[0], readout_ref[1]], axis=0), (1, 0)
    )
    low = readout_turned[pl.ds(2 * me, 1), :]
    high = readout_turned[pl.ds(2 * me + 1, 1), :]
    readout = (
        jnp.where(left, low, pltpu.roll(high, STATES, 1)),
        jnp.where(left, pltpu.roll(low, STATES, 1), high),
    )
    primal = primal_rows(step_row, decay_row, turn_row, readout)
    offsets = lax.broadcasted_iota(jnp.int32, (WIDTH, WIDTH), 0).astype(jnp.float32)
    starts = offsets * float(WIDTH)
    near = power_table(primal["rate"], offsets)
    base = power_table(primal["rate"], starts)
    tables = halves(
        jnp.concatenate([near[0], near[1], offsets * near[0], offsets * near[1]], axis=1)
    )
    for copy in loads:
        copy.wait()

    own.wait()
    rest = arrived.at[:, pl.ds(0, OWNERS - 1)]
    pltpu.make_async_copy(rest, rest, signal_sem).wait()
    signals = jnp.concatenate(
        [arrived.reshape(2, 2 * OWNERS, WIDTH)[0], arrived.reshape(2, 2 * OWNERS, WIDTH)[1]],
        axis=1,
    )
    lags = correlate(signals, first, turns, second, third, fourth)
    lag_rows[:, 0, :] = lags[:, :WIDTH]
    lag_rows[:, 1, :] = lags[:, WIDTH:]

    powers, lag_powers = power_sums(lags, tables, base, starts, norm_scale)
    readout_grad, step_terms, state_grad = parameter_rows(primal, readout, powers, lag_powers)
    cross_rows[...] = jnp.where(
        left,
        state_grad[0] + pltpu.roll(state_grad[0], STATES, 1),
        state_grad[1] + pltpu.roll(state_grad[1], STATES, 1),
    )
    readout_rows[0] = readout_grad[0]
    readout_rows[1] = readout_grad[1]
    cross_in[row] = cross_rows[...]
    for other in rows_across:
        send(cross_rows, cross_in.at[row], send_sem.at[3], cross_sem, {"ch": other})
    own_readout = pltpu.make_async_copy(readout_rows, readout_out.at[:, me], own_sem.at[1])
    own_readout.start()
    own_lags = pltpu.make_async_copy(lag_rows.at[me], lags_out.at[me], own_sem.at[2])
    own_lags.start()
    per_peer(
        me,
        lambda peer: send(
            lag_rows.at[peer], lags_out.at[me], send_sem.at[1], lag_sem, {"seq": peer}
        ),
    )

    first_step = jnp.sum(jnp.where(left, step_terms, 0.0), axis=1, keepdims=True)
    second_step = jnp.sum(jnp.where(left, 0.0, step_terms), axis=1, keepdims=True)
    count = WIDTH * lax.broadcasted_iota(jnp.int32, (2, WIDTH), 0) + lax.broadcasted_iota(
        jnp.int32, (2, WIDTH), 1
    )
    line_rows[0:2, :] = jnp.where(
        count == 2 * me, first_step, jnp.where(count == 2 * me + 1, second_step, 0.0)
    )
    part = cross_in.at[pl.ds(0, 3)]
    pltpu.make_async_copy(part, part, cross_sem).wait()
    line_rows[2:3, :] = (cross_in[0] + cross_in[1]) + (cross_in[2] + cross_in[3])
    line_rows[3:4, :] = jnp.zeros_like(step_row)
    line_in[2 * y + core] = line_rows[...]
    line = [
        16 * at_y + 2 * z + at_core
        for at_y in ring_places(y, 8)
        for at_core in (1 - core, core)
    ]
    for peer in line[:-1]:
        send(line_rows, line_in.at[2 * y + core], send_sem.at[4], line_sem, {"seq": peer})
    per_peer(
        me,
        lambda peer: send(
            readout_rows, readout_out.at[:, me], send_sem.at[2], readout_sem, {"seq": peer}
        ),
    )
    part = line_in.at[pl.ds(0, 15)]
    pltpu.make_async_copy(part, part, line_sem).wait()
    column_rows[...] = sum_in_order(line_in, 16)
    column_in[z] = column_rows[...]
    for at_z in ring_places(z, 8)[:7]:
        send(
            column_rows,
            column_in.at[z],
            send_sem.at[5],
            column_sem,
            {"seq": 16 * y + 2 * at_z + core},
        )
    part = column_in.at[pl.ds(0, 7)]
    pltpu.make_async_copy(part, part, column_sem).wait()
    sums_out[...] = sum_in_order(column_in, 8)

    own_lags.wait()
    own_readout.wait()
    part = lags_out.at[pl.ds(0, OWNERS - 1)]
    pltpu.make_async_copy(part, part, lag_sem).wait()
    pltpu.make_async_copy(part, part, send_sem.at[1]).wait()
    part = readout_out.at[:, pl.ds(0, OWNERS - 1)]
    pltpu.make_async_copy(part, part, readout_sem).wait()
    pltpu.make_async_copy(part, part, send_sem.at[2]).wait()
    pltpu.make_async_copy(rest, rest, send_sem.at[0]).wait()
    for buffer, count_sent, place in ((cross_in, 3, 3), (line_in, 15, 4), (column_in, 7, 5)):
        part = buffer.at[pl.ds(0, count_sent)]
        pltpu.make_async_copy(part, part, send_sem.at[place]).wait()


def sum_in_order(buffer, count):
    parts = [buffer[place] for place in range(count)]
    while len(parts) > 1:
        parts = [parts[place] + parts[place + 1] for place in range(0, len(parts), 2)]
    return parts[0]


def finish(lags_ref, readout_ref, sums_ref, lags_out, readout_out, step_out, state_out):
    lags_out[...] = lags_ref[...]
    blocks = []
    for part in range(2):
        turned = jnp.transpose(readout_ref[part], (1, 0))
        blocks.append(jnp.concatenate([turned[:STATES], turned[STATES:]], axis=1))
    value = jnp.concatenate(blocks, axis=0)
    at_row = lax.broadcasted_iota(jnp.int32, (2 * OWNERS, 2 * OWNERS), 0)
    at_column = lax.broadcasted_iota(jnp.int32, (2 * OWNERS, 2 * OWNERS), 1)
    places = 2 * (at_row % OWNERS) + at_row // OWNERS
    order = jnp.where(at_column == places, 1.0, 0.0).astype(jnp.bfloat16)
    high = value.astype(jnp.bfloat16)
    left = value - high.astype(jnp.float32)
    middle, low = halves(left)
    sorted_ = dot(high, order) + (dot(middle, order) + dot(low, order))
    readout_out[0] = sorted_[:STATES]
    readout_out[1] = sorted_[STATES:]
    step_out[...] = sums_ref[0:2, :]
    state_out[0:1, :] = sums_ref[2:3, :STATES]
    state_out[1:2, :] = sums_ref[2:3, STATES:]


def per_device(tables, inputs, out_grad, readout, log_step, decay_log, rotation):
    norm_scale = 1.0 / math.sqrt(LENGTH)
    dma = pltpu.SemaphoreType.DMA
    any_space = pl.BlockSpec(memory_space=pl.ANY)
    vmem = pl.BlockSpec(memory_space=pltpu.VMEM)
    smem = pl.BlockSpec(memory_space=pltpu.SMEM)
    f32 = jnp.float32
    lags, readout_rows, sums = pl.pallas_call(
        functools.partial(kernel, norm_scale),
        out_shape=(
            jax.ShapeDtypeStruct((OWNERS, 2, WIDTH), f32),
            jax.ShapeDtypeStruct((2, OWNERS, 1, WIDTH), f32),
            jax.ShapeDtypeStruct((4, WIDTH), f32),
        ),
        in_specs=[any_space, any_space, vmem, smem, vmem, vmem] + [any_space] * 5,
        out_specs=(vmem, vmem, vmem),
        scratch_shapes=[
            pltpu.VMEM((2, OWNERS, 2, WIDTH), jnp.bfloat16),
            pltpu.VMEM((2, OWNERS, 2, WIDTH), jnp.bfloat16),
            pltpu.VMEM((OWNERS, 2, WIDTH), f32),
            pltpu.VMEM((2, 1, WIDTH), f32),
            pltpu.VMEM((2 * OWNERS, WIDTH), f32),
            pltpu.VMEM((1, WIDTH), f32),
            pltpu.VMEM((4, 1, WIDTH), f32),
            pltpu.VMEM((4, WIDTH), f32),
            pltpu.VMEM((16, 4, WIDTH), f32),
            pltpu.VMEM((4, WIDTH), f32),
            pltpu.VMEM((8, 4, WIDTH), f32),
        ]
        + [pltpu.VMEM(table.shape, table.dtype) for table in tables]
        + [dma((2,)), dma((5,)), dma((3,)), dma((6,)), dma, dma, dma, dma, dma, dma],
        compiler_params=pltpu.CompilerParams(collective_id=0, has_side_effects=True),
        name="channel_rows",
    )(
        inputs.reshape(OWNERS, 2, WIDTH),
        out_grad.reshape(OWNERS, 2, WIDTH),
        jnp.transpose(readout, (0, 2, 1)),
        log_step,
        decay_log.reshape(1, STATES),
        rotation.reshape(1, STATES),
        *[jnp.asarray(table) for table in tables],
    )
    kernel_grad, readout_grad, step_grad, state_grad = pl.pallas_call(
        finish,
        out_shape=(
            jax.ShapeDtypeStruct((2 * OWNERS, WIDTH), f32),
            jax.ShapeDtypeStruct((2, STATES, 2 * OWNERS), f32),
            jax.ShapeDtypeStruct((2, WIDTH), f32),
            jax.ShapeDtypeStruct((2, STATES), f32),
        ),
        in_specs=[vmem] * 3,
        out_specs=(vmem,) * 4,
        name="finish",
    )(
        lags.reshape(2 * OWNERS, WIDTH),
        readout_rows.reshape(2, OWNERS, WIDTH),
        sums,
    )
    return (
        kernel_grad,
        jnp.transpose(readout_grad, (0, 2, 1)),
        step_grad.reshape(2 * OWNERS),
        state_grad,
    )


def solution(mesh):
    tables = transform_tables()
    return jax.shard_map(
        functools.partial(per_device, tables),
        mesh=mesh,
        in_specs=(P("ch", "seq"), P("ch", "seq"), P(None, "ch", None), P("ch"), P(), P()),
        out_specs=(P("ch", "seq"), P(None, "ch", None), P("ch"), P()),
        check_vma=False,
    )
```

```python
import functools
import math

import jax
import jax.numpy as jnp
import numpy as np
from jax import lax
from jax.experimental import pallas as pl
from jax.experimental.pallas import tpu as pltpu
from jax.sharding import PartitionSpec as P

MESH = pl.DeviceIdType.MESH
OWNERS = 128
WIDTH = 128
LENGTH = OWNERS * WIDTH
STATES = 64


def split_table(table):
    high = np.asarray(table, np.float32).astype(jnp.bfloat16)
    low = (np.asarray(table, np.float64) - high.astype(np.float64)).astype(jnp.bfloat16)
    return np.stack([high, low])


def transform_tables():
    index = np.arange(WIDTH, dtype=np.float64)
    quarter = index + 0.25
    enter = 2.0 * np.pi * np.outer(quarter, index) / WIDTH
    spread = np.zeros((2, 2, WIDTH, OWNERS, 2))
    for channel in range(2):
        spread[0, channel, :, :, channel] = np.cos(enter)
        spread[1, channel, :, :, channel] = -np.sin(enter)
    first = spread.reshape(4 * WIDTH, 2 * OWNERS)
    turn = 2.0 * np.pi * np.outer(quarter, index) / LENGTH
    turns = np.stack([np.cos(turn), np.sin(turn)]).astype(np.float32)
    plain = 2.0 * np.pi * np.outer(index, index) / WIDTH
    cosine, sine = np.cos(plain), np.sin(plain)
    second = np.block([[cosine, -sine], [sine, cosine]])
    third = np.block([[cosine, sine], [-sine, cosine]])
    scale = 1.0 / (LENGTH * math.sqrt(LENGTH))
    leave = enter.T
    fourth = np.concatenate([np.cos(leave), -np.sin(leave)], axis=1) * scale
    return (
        split_table(first),
        turns,
        split_table(second),
        split_table(third),
        split_table(fourth),
    )


def dot(left, right):
    return jnp.dot(left, right, preferred_element_type=jnp.float32)


def halves(value):
    high = value.astype(jnp.bfloat16)
    return high, (value - high.astype(jnp.float32)).astype(jnp.bfloat16)


def dot_pair(left, right):
    return dot(left[0], right[0]) + (dot(left[0], right[1]) + dot(left[1], right[0]))


def sine_cosine(angle):
    turns = jnp.floor(angle * (2.0 / math.pi) + 0.5)
    rest = angle - turns * 1.5625
    rest = rest - turns * 0.0081787109375
    rest = rest - turns * 0.000116348266601562
    rest = rest - turns * 1.26759079665e-06
    square = rest * rest
    sine = rest + rest * square * (
        -1.6666667e-1 + square * (8.3333310e-3 + square * (-1.9840874e-4 + square * 2.7525562e-6))
    )
    cosine = (
        1.0
        - 0.5 * square
        + square
        * square
        * (4.16666667e-2 + square * (-1.38888889e-3 + square * (2.48015873e-5 - square * 2.7557319e-7)))
    )
    quadrant = turns - 4.0 * jnp.floor(turns * 0.25)
    odd = (quadrant == 1.0) | (quadrant == 3.0)
    sine_out = jnp.where(odd, cosine, sine)
    cosine_out = jnp.where(odd, sine, cosine)
    sine_out = jnp.where(quadrant >= 2.0, -sine_out, sine_out)
    cosine_out = jnp.where((quadrant == 1.0) | (quadrant == 2.0), -cosine_out, cosine_out)
    return sine_out, cosine_out


def exp_minus_one(value):
    series = 1.0 + value * (1.0 / 9.0)
    for count in (8.0, 7.0, 6.0, 5.0, 4.0, 3.0, 2.0):
        series = 1.0 + value * (1.0 / count) * series
    return jnp.where(jnp.abs(value) < 0.5, value * series, jnp.exp(value) - 1.0)


def multiply(left, right):
    return (left[0] * right[0] - left[1] * right[1], left[0] * right[1] + left[1] * right[0])


def conjugate(value):
    return (value[0], -value[1])


def primal_rows(step, decay, turn, readout):
    pole = (-jnp.exp(decay), turn)
    rate = (step * pole[0], step * pole[1])
    sine, cosine = sine_cosine(rate[1])
    half_sine, _ = sine_cosine(0.5 * rate[1])
    growth = jnp.exp(rate[0])
    lift = (
        exp_minus_one(rate[0]) * cosine - 2.0 * half_sine * half_sine,
        growth * sine,
    )
    norm = pole[0] * pole[0] + pole[1] * pole[1]
    inverse = (pole[0] / norm, -pole[1] / norm)
    ratio = multiply(lift, inverse)
    coef = multiply(readout, ratio)
    power = (growth * cosine, growth * sine)
    return dict(
        step=step, pole=pole, rate=rate, inverse=inverse, ratio=ratio, coef=coef, power=power
    )


def power_table(rate, positions):
    decays = jnp.exp(rate[0] * positions)
    sine, cosine = sine_cosine(rate[1] * positions)
    return decays * cosine, decays * sine


def correlate(signals, first, turns, second, third, fourth):
    spread = dot(first[0], signals) + dot(first[1], signals)
    turn_cos, turn_sin = turns[0], turns[1]
    blocks = []
    for channel in range(2):
        for signal in range(2):
            columns = slice(signal * WIDTH, (signal + 1) * WIDTH)
            real = spread[channel * WIDTH : (channel + 1) * WIDTH, columns]
            imag = spread[(2 + channel) * WIDTH : (3 + channel) * WIDTH, columns]
            blocks.append(
                jnp.concatenate(
                    [real * turn_cos + imag * turn_sin, imag * turn_cos - real * turn_sin], axis=1
                )
            )
    spectrum = dot_pair(halves(jnp.concatenate(blocks, axis=0)), second)
    products = []
    for channel in range(2):
        entry = spectrum[2 * channel * WIDTH : (2 * channel + 1) * WIDTH]
        exit_ = spectrum[(2 * channel + 1) * WIDTH : (2 * channel + 2) * WIDTH]
        in_real, in_imag = entry[:, :WIDTH], entry[:, WIDTH:]
        out_real, out_imag = exit_[:, :WIDTH], exit_[:, WIDTH:]
        products.append(
            jnp.concatenate(
                [
                    out_real * in_real + out_imag * in_imag,
                    out_imag * in_real - out_real * in_imag,
                ],
                axis=1,
            )
        )
    back = dot_pair(halves(jnp.concatenate(products, axis=0)), third)
    columns = []
    for channel in range(2):
        real = back[channel * WIDTH : (channel + 1) * WIDTH, :WIDTH]
        imag = back[channel * WIDTH : (channel + 1) * WIDTH, WIDTH:]
        columns.append(
            jnp.concatenate(
                [real * turn_cos - imag * turn_sin, real * turn_sin + imag * turn_cos], axis=0
            )
        )
    return dot_pair((fourth[0], fourth[1]), halves(jnp.concatenate(columns, axis=1)))


def sum_rows(value):
    return jnp.sum(value, axis=0, keepdims=True)


def power_sums(lags, tables, base, starts, norm_scale):
    stacked = jnp.concatenate([lags[:, :WIDTH], lags[:, WIDTH:]], axis=0)
    raw = dot_pair(halves(stacked), tables)
    lane = lax.broadcasted_iota(jnp.int32, (OWNERS, WIDTH), 1)
    picked = [
        jnp.where(
            lane < STATES,
            raw[:OWNERS, part * WIDTH : (part + 1) * WIDTH],
            raw[OWNERS:, part * WIDTH : (part + 1) * WIDTH],
        )
        for part in range(4)
    ]
    plain = (picked[0], picked[1])
    lagged = (starts * picked[0] + picked[2], starts * picked[1] + picked[3])
    powers = multiply(base, plain)
    lag_powers = multiply(base, lagged)
    return (
        (norm_scale * sum_rows(powers[0]), norm_scale * sum_rows(powers[1])),
        (norm_scale * sum_rows(lag_powers[0]), norm_scale * sum_rows(lag_powers[1])),
    )


def parameter_rows(primal, readout, powers, lag_powers):
    coef_grad = (2.0 * powers[0], -2.0 * powers[1])
    readout_grad = multiply(conjugate(primal["ratio"]), coef_grad)
    ratio_grad = multiply(conjugate(readout), coef_grad)
    shifted = multiply(primal["coef"], lag_powers)
    lift_grad = multiply(conjugate(primal["inverse"]), ratio_grad)
    through = multiply(conjugate(primal["power"]), lift_grad)
    rate_grad = (2.0 * shifted[0] + through[0], -2.0 * shifted[1] + through[1])
    direct = multiply(conjugate(primal["ratio"]), lift_grad)
    step, pole = primal["step"], primal["pole"]
    pole_grad = (step * rate_grad[0] - direct[0], step * rate_grad[1] - direct[1])
    step_terms = step * (rate_grad[0] * pole[0] + rate_grad[1] * pole[1])
    return readout_grad, step_terms, (pole_grad[0] * pole[0], pole_grad[1])


def offset_of(place, ring):
    return ring // 2 + (1 - 2 * (place % 2)) * ((place + 1) // 2)


def place_of(me):
    return me // 16, (me // 2) % 8, me % 2


def ring_places(place, ring):
    return [(place + offset_of(count, ring)) % ring for count in range(ring)]


def per_peer(me, action):
    y, z, core = place_of(me)
    to_y = [16 * other for other in ring_places(y, 8)]
    to_z = [2 * other for other in ring_places(z, 8)]
    to_core = [1 - core, core]
    peers = [at_y + at_z + at_core for at_y in to_y for at_z in to_z for at_core in to_core]
    for peer in peers[:-1]:
        action(peer)


def kernel(
    norm_scale,
    inputs_ref,
    grads_ref,
    readout_in,
    log_step_in,
    decay_in,
    rotation_in,
    first_ref,
    turns_ref,
    second_ref,
    third_ref,
    fourth_ref,
    lags_out,
    readout_out,
    sums_out,
    outgoing,
    arrived,
    lag_rows,
    readout_rows,
    readout_turned,
    cross_rows,
    cross_in,
    line_rows,
    line_in,
    column_rows,
    column_in,
    readout_ref,
    log_step_ref,
    decay_ref,
    rotation_ref,
    first,
    turns,
    second,
    third,
    fourth,
    stage_sem,
    table_sem,
    own_sem,
    send_sem,
    signal_sem,
    lag_sem,
    readout_sem,
    cross_sem,
    line_sem,
    column_sem,
):
    me = lax.axis_index("seq")
    row = lax.axis_index("ch")
    y, z, core = place_of(me)
    stages = [
        pltpu.make_async_copy(inputs_ref, outgoing.at[0], stage_sem.at[0]),
        pltpu.make_async_copy(grads_ref, outgoing.at[1], stage_sem.at[1]),
    ]
    for copy in stages:
        copy.start()
    barrier = pltpu.get_barrier_semaphore()

    def greet(peer):
        pl.semaphore_signal(barrier, inc=1, device_id={"seq": peer}, device_id_type=MESH)

    per_peer(me, greet)
    rows_across = [(row + step) % 4 for step in range(1, 4)]
    for other in rows_across:
        pl.semaphore_signal(barrier, inc=1, device_id={"ch": other}, device_id_type=MESH)
    loads = [
        pltpu.make_async_copy(source, target, table_sem.at[place])
        for place, (source, target) in enumerate(
            (
                (log_step_in, log_step_ref),
                (decay_in, decay_ref),
                (rotation_in, rotation_ref),
                (readout_in, readout_ref),
                (first_ref, first),
                (turns_ref, turns),
                (second_ref, second),
                (third_ref, third),
                (fourth_ref, fourth),
            )
        )
    ]
    for copy in loads:
        copy.start()
    for copy in stages:
        copy.wait()
    pl.semaphore_wait(barrier, OWNERS - 1 + 3)

    def send(source, target, sent, received, device):
        pltpu.make_async_remote_copy(
            src_ref=source,
            dst_ref=target,
            send_sem=sent,
            recv_sem=received,
            device_id=device,
            device_id_type=MESH,
        ).start()

    own = pltpu.make_async_copy(outgoing.at[:, me], arrived.at[:, me], own_sem.at[0])
    own.start()
    per_peer(
        me,
        lambda peer: send(
            outgoing.at[:, peer], arrived.at[:, me], send_sem.at[0], signal_sem, {"seq": peer}
        ),
    )

    for copy in loads[:4]:
        copy.wait()
    lane_row = lax.broadcasted_iota(jnp.int32, (1, WIDTH), 1)
    left = lane_row < STATES
    step_row = jnp.exp(jnp.where(left, log_step_ref[2 * me], log_step_ref[2 * me + 1]))
    decay_row = jnp.concatenate([decay_ref[...], decay_ref[...]], axis=1)
    turn_row = jnp.concatenate([rotation_ref[...], rotation_ref[...]], axis=1)
    readout_turned[...] = jnp.transpose(
        jnp.concatenate([readout_ref[0], readout_ref[1]], axis=0), (1, 0)
    )
    low = readout_turned[pl.ds(2 * me, 1), :]
    high = readout_turned[pl.ds(2 * me + 1, 1), :]
    readout = (
        jnp.where(left, low, pltpu.roll(high, STATES, 1)),
        jnp.where(left, pltpu.roll(low, STATES, 1), high),
    )
    primal = primal_rows(step_row, decay_row, turn_row, readout)
    offsets = lax.broadcasted_iota(jnp.int32, (WIDTH, WIDTH), 0).astype(jnp.float32)
    starts = offsets * float(WIDTH)
    near = power_table(primal["rate"], offsets)
    base = power_table(primal["rate"], starts)
    tables = halves(
        jnp.concatenate([near[0], near[1], offsets * near[0], offsets * near[1]], axis=1)
    )
    for copy in loads[4:]:
        copy.wait()

    own.wait()
    rest = arrived.at[:, pl.ds(0, OWNERS - 1)]
    pltpu.make_async_copy(rest, rest, signal_sem).wait()
    signals = jnp.concatenate(
        [arrived.reshape(2, 2 * OWNERS, WIDTH)[0], arrived.reshape(2, 2 * OWNERS, WIDTH)[1]],
        axis=1,
    )
    lags = correlate(signals, first, turns, second, third, fourth)
    lag_rows[:, 0, :] = lags[:, :WIDTH]
    lag_rows[:, 1, :] = lags[:, WIDTH:]

    powers, lag_powers = power_sums(lags, tables, base, starts, norm_scale)
    readout_grad, step_terms, state_grad = parameter_rows(primal, readout, powers, lag_powers)
    cross_rows[...] = jnp.where(
        left,
        state_grad[0] + pltpu.roll(state_grad[0], STATES, 1),
        state_grad[1] + pltpu.roll(state_grad[1], STATES, 1),
    )
    readout_rows[0] = readout_grad[0]
    readout_rows[1] = readout_grad[1]
    cross_in[row] = cross_rows[...]
    for other in rows_across:
        send(cross_rows, cross_in.at[row], send_sem.at[3], cross_sem, {"ch": other})
    readout_out[0, y, z, core] = readout_grad[0]
    readout_out[1, y, z, core] = readout_grad[1]
    around_y = ring_places(y, 8)
    around_z = ring_places(z, 8)
    for at_y in around_y[:-1]:
        send(
            readout_rows.at[0],
            readout_out.at[0, y, z, core],
            send_sem.at[2],
            readout_sem.at[0],
            {"seq": 16 * at_y + 2 * z + core},
        )
    for at_z in around_z[:-1]:
        send(
            readout_rows.at[1],
            readout_out.at[1, y, z, core],
            send_sem.at[6],
            readout_sem.at[1],
            {"seq": 16 * y + 2 * at_z + core},
        )
    own_lags = pltpu.make_async_copy(lag_rows.at[me], lags_out.at[me], own_sem.at[1])
    own_lags.start()
    per_peer(
        me,
        lambda peer: send(
            lag_rows.at[peer], lags_out.at[me], send_sem.at[1], lag_sem, {"seq": peer}
        ),
    )

    first_step = jnp.sum(jnp.where(left, step_terms, 0.0), axis=1, keepdims=True)
    second_step = jnp.sum(jnp.where(left, 0.0, step_terms), axis=1, keepdims=True)
    count = WIDTH * lax.broadcasted_iota(jnp.int32, (2, WIDTH), 0) + lax.broadcasted_iota(
        jnp.int32, (2, WIDTH), 1
    )
    line_rows[0:2, :] = jnp.where(
        count == 2 * me, first_step, jnp.where(count == 2 * me + 1, second_step, 0.0)
    )
    part = cross_in.at[pl.ds(0, 3)]
    pltpu.make_async_copy(part, part, cross_sem).wait()
    line_rows[2:3, :] = (cross_in[0] + cross_in[1]) + (cross_in[2] + cross_in[3])
    line_rows[3:4, :] = jnp.zeros_like(step_row)
    line_in[2 * y + core] = line_rows[...]
    line = [16 * at_y + 2 * z + at_core for at_y in around_y for at_core in (1 - core, core)]
    column = [16 * y + 2 * at_z + at_core for at_z in around_z for at_core in (1 - core, core)]
    for peer in line[:-1]:
        send(line_rows, line_in.at[2 * y + core], send_sem.at[4], line_sem, {"seq": peer})
    real_line = readout_out.at[0, :, z, core]
    imag_line = readout_out.at[1, y, :, core]
    real_seven = readout_out.at[0, pl.ds(0, 7), 0, 0]
    pltpu.make_async_copy(real_seven, real_seven, readout_sem.at[0]).wait()
    for peer in column[:-1]:
        send(real_line, real_line, send_sem.at[7], readout_sem.at[2], {"seq": peer})
    pltpu.make_async_copy(real_seven, real_seven, readout_sem.at[1]).wait()
    for peer in line[:-1]:
        send(imag_line, imag_line, send_sem.at[8], readout_sem.at[3], {"seq": peer})
    part = line_in.at[pl.ds(0, 15)]
    pltpu.make_async_copy(part, part, line_sem).wait()
    column_rows[...] = sum_in_order(line_in, 16)
    column_in[z] = column_rows[...]
    for at_z in around_z[:-1]:
        send(
            column_rows,
            column_in.at[z],
            send_sem.at[5],
            column_sem,
            {"seq": 16 * y + 2 * at_z + core},
        )
    part = column_in.at[pl.ds(0, 7)]
    pltpu.make_async_copy(part, part, column_sem).wait()
    sums_out[...] = sum_in_order(column_in, 8)

    own_lags.wait()
    part = lags_out.at[pl.ds(0, OWNERS - 1)]
    pltpu.make_async_copy(part, part, lag_sem).wait()
    pltpu.make_async_copy(part, part, send_sem.at[1]).wait()
    part = readout_out.at[0].reshape(16, 8, 1, WIDTH).at[pl.ds(0, 15)]
    pltpu.make_async_copy(part, part, readout_sem.at[2]).wait()
    pltpu.make_async_copy(part, part, readout_sem.at[3]).wait()
    pltpu.make_async_copy(part, part, send_sem.at[7]).wait()
    pltpu.make_async_copy(part, part, send_sem.at[8]).wait()
    pltpu.make_async_copy(real_seven, real_seven, send_sem.at[2]).wait()
    pltpu.make_async_copy(real_seven, real_seven, send_sem.at[6]).wait()
    pltpu.make_async_copy(rest, rest, send_sem.at[0]).wait()
    for buffer, count_sent, place in ((cross_in, 3, 3), (line_in, 15, 4), (column_in, 7, 5)):
        part = buffer.at[pl.ds(0, count_sent)]
        pltpu.make_async_copy(part, part, send_sem.at[place]).wait()


def sum_in_order(buffer, count):
    parts = [buffer[place] for place in range(count)]
    while len(parts) > 1:
        parts = [parts[place] + parts[place + 1] for place in range(0, len(parts), 2)]
    return parts[0]


def finish(
    lags_ref, readout_ref, sums_ref, lags_out, readout_out, step_out, state_out, lag_sem
):
    lags = pltpu.make_async_copy(lags_ref, lags_out, lag_sem)
    lags.start()
    blocks = []
    for part in range(2):
        turned = jnp.transpose(readout_ref[part], (1, 0))
        blocks.append(jnp.concatenate([turned[:STATES], turned[STATES:]], axis=1))
    value = jnp.concatenate(blocks, axis=0)
    at_row = lax.broadcasted_iota(jnp.int32, (2 * OWNERS, 2 * OWNERS), 0)
    at_column = lax.broadcasted_iota(jnp.int32, (2 * OWNERS, 2 * OWNERS), 1)
    places = 2 * (at_row % OWNERS) + at_row // OWNERS
    order = jnp.where(at_column == places, 1.0, 0.0).astype(jnp.bfloat16)
    high = value.astype(jnp.bfloat16)
    left = value - high.astype(jnp.float32)
    middle, low = halves(left)
    sorted_ = dot(high, order) + (dot(middle, order) + dot(low, order))
    readout_out[0] = sorted_[:STATES]
    readout_out[1] = sorted_[STATES:]
    step_out[...] = sums_ref[0:2, :]
    state_out[0:1, :] = sums_ref[2:3, :STATES]
    state_out[1:2, :] = sums_ref[2:3, STATES:]
    lags.wait()


def keep(value):
    return pltpu.with_memory_space_constraint(value, pltpu.VMEM)


def per_device(tables, inputs, out_grad, readout, log_step, decay_log, rotation):
    norm_scale = 1.0 / math.sqrt(LENGTH)
    dma = pltpu.SemaphoreType.DMA
    any_space = pl.BlockSpec(memory_space=pl.ANY)
    vmem = pl.BlockSpec(memory_space=pltpu.VMEM)
    f32 = jnp.float32
    lags, readout_rows, sums = pl.pallas_call(
        functools.partial(kernel, norm_scale),
        out_shape=(
            pltpu.VMEM((OWNERS, 2, WIDTH), f32),
            pltpu.VMEM((2, 8, 8, 2, 1, WIDTH), f32),
            pltpu.VMEM((4, WIDTH), f32),
        ),
        in_specs=[any_space] * 11,
        out_specs=(vmem, vmem, vmem),
        scratch_shapes=[
            pltpu.VMEM((2, OWNERS, 2, WIDTH), jnp.bfloat16),
            pltpu.VMEM((2, OWNERS, 2, WIDTH), jnp.bfloat16),
            pltpu.VMEM((OWNERS, 2, WIDTH), f32),
            pltpu.VMEM((2, 1, WIDTH), f32),
            pltpu.VMEM((2 * OWNERS, WIDTH), f32),
            pltpu.VMEM((1, WIDTH), f32),
            pltpu.VMEM((4, 1, WIDTH), f32),
            pltpu.VMEM((4, WIDTH), f32),
            pltpu.VMEM((16, 4, WIDTH), f32),
            pltpu.VMEM((4, WIDTH), f32),
            pltpu.VMEM((8, 4, WIDTH), f32),
        ]
        + [
            pltpu.VMEM((2, STATES, 2 * OWNERS), f32),
            pltpu.SMEM((2 * OWNERS,), f32),
            pltpu.VMEM((1, STATES), f32),
            pltpu.VMEM((1, STATES), f32),
        ]
        + [pltpu.VMEM(table.shape, table.dtype) for table in tables]
        + [dma((2,)), dma((9,)), dma((2,)), dma((9,)), dma, dma, dma((4,)), dma, dma, dma],
        compiler_params=pltpu.CompilerParams(collective_id=0, has_side_effects=True),
        name="channel_rows",
    )(
        inputs.reshape(OWNERS, 2, WIDTH),
        out_grad.reshape(OWNERS, 2, WIDTH),
        jnp.transpose(readout, (0, 2, 1)),
        log_step,
        decay_log.reshape(1, STATES),
        rotation.reshape(1, STATES),
        *[jnp.asarray(table) for table in tables],
    )
    kernel_grad, readout_grad, step_grad, state_grad = pl.pallas_call(
        finish,
        out_shape=(
            jax.ShapeDtypeStruct((2 * OWNERS, WIDTH), f32),
            jax.ShapeDtypeStruct((2, STATES, 2 * OWNERS), f32),
            jax.ShapeDtypeStruct((2, WIDTH), f32),
            jax.ShapeDtypeStruct((2, STATES), f32),
        ),
        in_specs=[vmem] * 3,
        out_specs=(any_space, vmem, vmem, vmem),
        scratch_shapes=[dma],
        name="finish",
    )(
        keep(lags.reshape(2 * OWNERS, WIDTH)),
        keep(readout_rows.reshape(2, OWNERS, WIDTH)),
        keep(sums),
    )
    return (
        kernel_grad,
        jnp.transpose(readout_grad, (0, 2, 1)),
        step_grad.reshape(2 * OWNERS),
        state_grad,
    )


def solution(mesh):
    tables = transform_tables()
    return jax.shard_map(
        functools.partial(per_device, tables),
        mesh=mesh,
        in_specs=(P("ch", "seq"), P("ch", "seq"), P(None, "ch", None), P("ch"), P(), P()),
        out_specs=(P("ch", "seq"), P(None, "ch", None), P("ch"), P()),
        check_vma=False,
    )
```

```python
import functools
import math

import jax
import jax.numpy as jnp
import numpy as np
from jax import lax
from jax.experimental import pallas as pl
from jax.experimental.pallas import tpu as pltpu
from jax.sharding import PartitionSpec as P

MESH = pl.DeviceIdType.MESH
OWNERS = 128
WIDTH = 128
LENGTH = OWNERS * WIDTH
STATES = 64


def split_table(table):
    high = np.asarray(table, np.float32).astype(jnp.bfloat16)
    low = (np.asarray(table, np.float64) - high.astype(np.float64)).astype(jnp.bfloat16)
    return np.stack([high, low])


def transform_tables():
    index = np.arange(WIDTH, dtype=np.float64)
    quarter = index + 0.25
    enter = 2.0 * np.pi * np.outer(quarter, index) / WIDTH
    spread = np.zeros((2, 2, WIDTH, OWNERS, 2))
    for channel in range(2):
        spread[0, channel, :, :, channel] = np.cos(enter)
        spread[1, channel, :, :, channel] = -np.sin(enter)
    first = spread.reshape(4 * WIDTH, 2 * OWNERS)
    turn = 2.0 * np.pi * np.outer(quarter, index) / LENGTH
    turns = np.stack([np.cos(turn), np.sin(turn)]).astype(np.float32)
    plain = 2.0 * np.pi * np.outer(index, index) / WIDTH
    cosine, sine = np.cos(plain), np.sin(plain)
    second = np.block([[cosine, -sine], [sine, cosine]])
    third = np.block([[cosine, sine], [-sine, cosine]])
    scale = 1.0 / (LENGTH * math.sqrt(LENGTH))
    leave = enter.T
    fourth = np.concatenate([np.cos(leave), -np.sin(leave)], axis=1) * scale
    return (
        split_table(first),
        turns,
        split_table(second),
        split_table(third),
        split_table(fourth),
    )


def dot(left, right):
    return jnp.dot(left, right, preferred_element_type=jnp.float32)


def halves(value):
    high = value.astype(jnp.bfloat16)
    return high, (value - high.astype(jnp.float32)).astype(jnp.bfloat16)


def dot_pair(left, right):
    return dot(left[0], right[0]) + (dot(left[0], right[1]) + dot(left[1], right[0]))


def sine_cosine(angle):
    turns = jnp.floor(angle * (2.0 / math.pi) + 0.5)
    rest = angle - turns * 1.5625
    rest = rest - turns * 0.0081787109375
    rest = rest - turns * 0.000116348266601562
    rest = rest - turns * 1.26759079665e-06
    square = rest * rest
    sine = rest + rest * square * (
        -1.6666667e-1 + square * (8.3333310e-3 + square * (-1.9840874e-4 + square * 2.7525562e-6))
    )
    cosine = (
        1.0
        - 0.5 * square
        + square
        * square
        * (4.16666667e-2 + square * (-1.38888889e-3 + square * (2.48015873e-5 - square * 2.7557319e-7)))
    )
    quadrant = turns - 4.0 * jnp.floor(turns * 0.25)
    odd = (quadrant == 1.0) | (quadrant == 3.0)
    sine_out = jnp.where(odd, cosine, sine)
    cosine_out = jnp.where(odd, sine, cosine)
    sine_out = jnp.where(quadrant >= 2.0, -sine_out, sine_out)
    cosine_out = jnp.where((quadrant == 1.0) | (quadrant == 2.0), -cosine_out, cosine_out)
    return sine_out, cosine_out


def exp_minus_one(value):
    series = 1.0 + value * (1.0 / 9.0)
    for count in (8.0, 7.0, 6.0, 5.0, 4.0, 3.0, 2.0):
        series = 1.0 + value * (1.0 / count) * series
    return jnp.where(jnp.abs(value) < 0.5, value * series, jnp.exp(value) - 1.0)


def multiply(left, right):
    return (left[0] * right[0] - left[1] * right[1], left[0] * right[1] + left[1] * right[0])


def conjugate(value):
    return (value[0], -value[1])


def primal_rows(step, decay, turn, readout):
    pole = (-jnp.exp(decay), turn)
    rate = (step * pole[0], step * pole[1])
    sine, cosine = sine_cosine(rate[1])
    half_sine, _ = sine_cosine(0.5 * rate[1])
    growth = jnp.exp(rate[0])
    lift = (
        exp_minus_one(rate[0]) * cosine - 2.0 * half_sine * half_sine,
        growth * sine,
    )
    norm = pole[0] * pole[0] + pole[1] * pole[1]
    inverse = (pole[0] / norm, -pole[1] / norm)
    ratio = multiply(lift, inverse)
    coef = multiply(readout, ratio)
    power = (growth * cosine, growth * sine)
    return dict(
        step=step, pole=pole, rate=rate, inverse=inverse, ratio=ratio, coef=coef, power=power
    )


def power_table(rate, positions):
    decays = jnp.exp(rate[0] * positions)
    sine, cosine = sine_cosine(rate[1] * positions)
    return decays * cosine, decays * sine


def correlate(signals, first, turns, second, third, fourth):
    spread = dot(first[0], signals) + dot(first[1], signals)
    turn_cos, turn_sin = turns[0], turns[1]
    blocks = []
    for channel in range(2):
        for signal in range(2):
            columns = slice(signal * WIDTH, (signal + 1) * WIDTH)
            real = spread[channel * WIDTH : (channel + 1) * WIDTH, columns]
            imag = spread[(2 + channel) * WIDTH : (3 + channel) * WIDTH, columns]
            blocks.append(
                jnp.concatenate(
                    [real * turn_cos + imag * turn_sin, imag * turn_cos - real * turn_sin], axis=1
                )
            )
    spectrum = dot_pair(halves(jnp.concatenate(blocks, axis=0)), second)
    products = []
    for channel in range(2):
        entry = spectrum[2 * channel * WIDTH : (2 * channel + 1) * WIDTH]
        exit_ = spectrum[(2 * channel + 1) * WIDTH : (2 * channel + 2) * WIDTH]
        in_real, in_imag = entry[:, :WIDTH], entry[:, WIDTH:]
        out_real, out_imag = exit_[:, :WIDTH], exit_[:, WIDTH:]
        products.append(
            jnp.concatenate(
                [
                    out_real * in_real + out_imag * in_imag,
                    out_imag * in_real - out_real * in_imag,
                ],
                axis=1,
            )
        )
    back = dot_pair(halves(jnp.concatenate(products, axis=0)), third)
    columns = []
    for channel in range(2):
        real = back[channel * WIDTH : (channel + 1) * WIDTH, :WIDTH]
        imag = back[channel * WIDTH : (channel + 1) * WIDTH, WIDTH:]
        columns.append(
            jnp.concatenate(
                [real * turn_cos - imag * turn_sin, real * turn_sin + imag * turn_cos], axis=0
            )
        )
    return dot_pair((fourth[0], fourth[1]), halves(jnp.concatenate(columns, axis=1)))


def sum_rows(value):
    return jnp.sum(value, axis=0, keepdims=True)


def power_sums(lags, tables, base, starts, norm_scale):
    stacked = jnp.concatenate([lags[:, :WIDTH], lags[:, WIDTH:]], axis=0)
    raw = dot_pair(halves(stacked), tables)
    lane = lax.broadcasted_iota(jnp.int32, (OWNERS, WIDTH), 1)
    picked = [
        jnp.where(
            lane < STATES,
            raw[:OWNERS, part * WIDTH : (part + 1) * WIDTH],
            raw[OWNERS:, part * WIDTH : (part + 1) * WIDTH],
        )
        for part in range(4)
    ]
    plain = (picked[0], picked[1])
    lagged = (starts * picked[0] + picked[2], starts * picked[1] + picked[3])
    powers = multiply(base, plain)
    lag_powers = multiply(base, lagged)
    return (
        (norm_scale * sum_rows(powers[0]), norm_scale * sum_rows(powers[1])),
        (norm_scale * sum_rows(lag_powers[0]), norm_scale * sum_rows(lag_powers[1])),
    )


def parameter_rows(primal, readout, powers, lag_powers):
    coef_grad = (2.0 * powers[0], -2.0 * powers[1])
    readout_grad = multiply(conjugate(primal["ratio"]), coef_grad)
    ratio_grad = multiply(conjugate(readout), coef_grad)
    shifted = multiply(primal["coef"], lag_powers)
    lift_grad = multiply(conjugate(primal["inverse"]), ratio_grad)
    through = multiply(conjugate(primal["power"]), lift_grad)
    rate_grad = (2.0 * shifted[0] + through[0], -2.0 * shifted[1] + through[1])
    direct = multiply(conjugate(primal["ratio"]), lift_grad)
    step, pole = primal["step"], primal["pole"]
    pole_grad = (step * rate_grad[0] - direct[0], step * rate_grad[1] - direct[1])
    step_terms = step * (rate_grad[0] * pole[0] + rate_grad[1] * pole[1])
    return readout_grad, step_terms, (pole_grad[0] * pole[0], pole_grad[1])


def offset_of(place, ring):
    return ring // 2 + (1 - 2 * (place % 2)) * ((place + 1) // 2)


def place_of(me):
    return me // 16, (me // 2) % 8, me % 2


def ring_places(place, ring):
    return [(place + offset_of(count, ring)) % ring for count in range(ring)]


def per_peer(me, action):
    y, z, core = place_of(me)
    to_y = [16 * other for other in ring_places(y, 8)]
    to_z = [2 * other for other in ring_places(z, 8)]
    to_core = [1 - core, core]
    peers = [at_y + at_z + at_core for at_y in to_y for at_z in to_z for at_core in to_core]
    for peer in peers[:-1]:
        action(peer)


def kernel(
    norm_scale,
    inputs_ref,
    grads_ref,
    readout_in,
    log_step_in,
    decay_in,
    rotation_in,
    first_ref,
    turns_ref,
    second_ref,
    third_ref,
    fourth_ref,
    lags_out,
    sorted_out,
    step_out,
    state_out,
    outgoing,
    arrived,
    lag_rows,
    readout_rows,
    readout_all,
    readout_turned,
    state_rows,
    state_in,
    step_rows,
    step_in,
    column_rows,
    column_in,
    readout_ref,
    log_step_ref,
    decay_ref,
    rotation_ref,
    first,
    turns,
    second,
    third,
    fourth,
    stage_sem,
    table_sem,
    own_sem,
    send_sem,
    signal_sem,
    lag_sem,
    readout_sem,
    state_sem,
    step_sem,
    column_sem,
):
    me = lax.axis_index("seq")
    row = lax.axis_index("ch")
    y, z, core = place_of(me)
    stages = [
        pltpu.make_async_copy(inputs_ref, outgoing.at[0], stage_sem.at[0]),
        pltpu.make_async_copy(grads_ref, outgoing.at[1], stage_sem.at[1]),
    ]
    for copy in stages:
        copy.start()
    barrier = pltpu.get_barrier_semaphore()

    def greet(peer):
        pl.semaphore_signal(barrier, inc=1, device_id={"seq": peer}, device_id_type=MESH)

    per_peer(me, greet)
    around_y = ring_places(y, 8)
    around_z = ring_places(z, 8)
    around_x = [(row + step) % 4 for step in (2, 1, 3, 0)]
    across = [(at_x, 16 * at_y + 2 * z + core) for at_x in around_x[:3] for at_y in around_y]
    for at_x, peer in across:
        pl.semaphore_signal(
            barrier, inc=1, device_id={"ch": at_x, "seq": peer}, device_id_type=MESH
        )
    loads = [
        pltpu.make_async_copy(source, target, table_sem.at[place])
        for place, (source, target) in enumerate(
            (
                (log_step_in, log_step_ref),
                (decay_in, decay_ref),
                (rotation_in, rotation_ref),
                (readout_in, readout_ref),
                (first_ref, first),
                (turns_ref, turns),
                (second_ref, second),
                (third_ref, third),
                (fourth_ref, fourth),
            )
        )
    ]
    for copy in loads:
        copy.start()
    for copy in stages:
        copy.wait()
    pl.semaphore_wait(barrier, OWNERS - 1 + len(across))

    def send(source, target, sent, received, device):
        pltpu.make_async_remote_copy(
            src_ref=source,
            dst_ref=target,
            send_sem=sent,
            recv_sem=received,
            device_id=device,
            device_id_type=MESH,
        ).start()

    own = pltpu.make_async_copy(outgoing.at[:, me], arrived.at[:, me], own_sem.at[0])
    own.start()
    per_peer(
        me,
        lambda peer: send(
            outgoing.at[:, peer], arrived.at[:, me], send_sem.at[0], signal_sem, {"seq": peer}
        ),
    )

    for copy in loads[:4]:
        copy.wait()
    lane_row = lax.broadcasted_iota(jnp.int32, (1, WIDTH), 1)
    left = lane_row < STATES
    step_row = jnp.exp(jnp.where(left, log_step_ref[2 * me], log_step_ref[2 * me + 1]))
    decay_row = jnp.concatenate([decay_ref[...], decay_ref[...]], axis=1)
    turn_row = jnp.concatenate([rotation_ref[...], rotation_ref[...]], axis=1)
    readout_turned[...] = jnp.transpose(
        jnp.concatenate([readout_ref[0], readout_ref[1]], axis=0), (1, 0)
    )
    low = readout_turned[pl.ds(2 * me, 1), :]
    high = readout_turned[pl.ds(2 * me + 1, 1), :]
    readout = (
        jnp.where(left, low, pltpu.roll(high, STATES, 1)),
        jnp.where(left, pltpu.roll(low, STATES, 1), high),
    )
    primal = primal_rows(step_row, decay_row, turn_row, readout)
    offsets = lax.broadcasted_iota(jnp.int32, (WIDTH, WIDTH), 0).astype(jnp.float32)
    starts = offsets * float(WIDTH)
    near = power_table(primal["rate"], offsets)
    base = power_table(primal["rate"], starts)
    tables = halves(
        jnp.concatenate([near[0], near[1], offsets * near[0], offsets * near[1]], axis=1)
    )
    for copy in loads[4:]:
        copy.wait()

    own.wait()
    rest = arrived.at[:, pl.ds(0, OWNERS - 1)]
    pltpu.make_async_copy(rest, rest, signal_sem).wait()
    signals = jnp.concatenate(
        [arrived.reshape(2, 2 * OWNERS, WIDTH)[0], arrived.reshape(2, 2 * OWNERS, WIDTH)[1]],
        axis=1,
    )
    lags = correlate(signals, first, turns, second, third, fourth)
    lag_rows[:, 0, :] = lags[:, :WIDTH]
    lag_rows[:, 1, :] = lags[:, WIDTH:]

    powers, lag_powers = power_sums(lags, tables, base, starts, norm_scale)
    readout_grad, step_terms, state_grad = parameter_rows(primal, readout, powers, lag_powers)
    state_rows[...] = jnp.where(
        left,
        state_grad[0] + pltpu.roll(state_grad[0], STATES, 1),
        state_grad[1] + pltpu.roll(state_grad[1], STATES, 1),
    )
    line = [16 * at_y + 2 * z + core for at_y in around_y[:-1]]
    for at_x, peer in across + [(around_x[3], peer) for peer in line]:
        send(
            state_rows,
            state_in.at[row, y],
            send_sem.at[3],
            state_sem,
            {"ch": at_x, "seq": peer},
        )
    state_in[row, y] = state_rows[...]
    first_step = jnp.sum(jnp.where(left, step_terms, 0.0), axis=1, keepdims=True)
    second_step = jnp.sum(jnp.where(left, 0.0, step_terms), axis=1, keepdims=True)
    count = WIDTH * lax.broadcasted_iota(jnp.int32, (2, WIDTH), 0) + lax.broadcasted_iota(
        jnp.int32, (2, WIDTH), 1
    )
    step_rows[...] = jnp.where(
        count == 2 * me, first_step, jnp.where(count == 2 * me + 1, second_step, 0.0)
    )
    step_in[y] = step_rows[...]
    readout_rows[0] = readout_grad[0]
    readout_rows[1] = readout_grad[1]
    readout_all[0, y, z, core] = readout_grad[0]
    readout_all[1, y, z, core] = readout_grad[1]
    for peer in line:
        send(
            readout_rows.at[0],
            readout_all.at[0, y, z, core],
            send_sem.at[2],
            readout_sem.at[0],
            {"seq": peer},
        )
    for at_z in around_z[:-1]:
        send(
            readout_rows.at[1],
            readout_all.at[1, y, z, core],
            send_sem.at[6],
            readout_sem.at[1],
            {"seq": 16 * y + 2 * at_z + core},
        )
    for peer in line:
        send(step_rows, step_in.at[y], send_sem.at[4], step_sem, {"seq": peer})
    own_lags = pltpu.make_async_copy(lag_rows.at[me], lags_out.at[me], own_sem.at[1])
    own_lags.start()
    per_peer(
        me,
        lambda peer: send(
            lag_rows.at[peer], lags_out.at[me], send_sem.at[1], lag_sem, {"seq": peer}
        ),
    )

    def await_bytes(part, *semaphores):
        for semaphore in semaphores:
            pltpu.make_async_copy(part, part, semaphore).wait()

    ends = [16 * at_y + 2 * z + at_core for at_y in around_y for at_core in (1 - core, core)]
    column = [16 * y + 2 * at_z + at_core for at_z in around_z for at_core in (1 - core, core)]
    real_line = readout_all.at[0, :, z, core]
    imag_line = readout_all.at[1, y, :, core]
    seven = readout_all.at[0, pl.ds(0, 7), 0, 0]
    await_bytes(seven, readout_sem.at[0])
    for peer in column[:-1]:
        send(real_line, real_line, send_sem.at[7], readout_sem.at[2], {"seq": peer})
    await_bytes(seven, readout_sem.at[1])
    for peer in ends[:-1]:
        send(imag_line, imag_line, send_sem.at[8], readout_sem.at[3], {"seq": peer})

    most = state_in.reshape(32, 1, WIDTH).at[pl.ds(0, 31)]
    await_bytes(most, state_sem)
    await_bytes(step_in.at[pl.ds(0, 7)], step_sem)
    column_rows[0:2, :] = sum_in_order(step_in, 8)
    column_rows[2:3, :] = sum_rows(state_in.reshape(32, WIDTH)[...])
    column_rows[3:4, :] = jnp.zeros_like(step_row)
    column_in[2 * z + core] = column_rows[...]
    for peer in column[:-1]:
        send(column_rows, column_in.at[2 * z + core], send_sem.at[5], column_sem, {"seq": peer})

    fifteen = readout_all.at[0].reshape(16, 8, 1, WIDTH).at[pl.ds(0, 15)]
    await_bytes(fifteen, readout_sem.at[2], readout_sem.at[3])
    sorted_ = sort_channels(readout_all.reshape(2, OWNERS, WIDTH))
    sorted_out[0] = sorted_[:STATES]
    sorted_out[1] = sorted_[STATES:]
    own_lags.wait()
    part = lags_out.at[pl.ds(0, OWNERS - 1)]
    await_bytes(part, lag_sem, send_sem.at[1])
    await_bytes(fifteen, send_sem.at[7], send_sem.at[8])
    await_bytes(seven, send_sem.at[2], send_sem.at[6])
    await_bytes(rest, send_sem.at[0])
    await_bytes(most, send_sem.at[3])
    await_bytes(step_in.at[pl.ds(0, 7)], send_sem.at[4])
    ended = column_in.at[pl.ds(0, 15)]
    await_bytes(ended, column_sem)
    sums = sum_in_order(column_in, 16)
    step_out[...] = sums[0:2, :]
    state_out[0:1, :] = sums[2:3, :STATES]
    state_out[1:2, :] = sums[2:3, STATES:]
    await_bytes(ended, send_sem.at[5])


def sum_in_order(buffer, count):
    parts = [buffer[place] for place in range(count)]
    while len(parts) > 1:
        parts = [parts[place] + parts[place + 1] for place in range(0, len(parts), 2)]
    return parts[0]


def sort_channels(rows_ref):
    blocks = []
    for part in range(2):
        turned = jnp.transpose(rows_ref[part], (1, 0))
        blocks.append(jnp.concatenate([turned[:STATES], turned[STATES:]], axis=1))
    value = jnp.concatenate(blocks, axis=0)
    at_row = lax.broadcasted_iota(jnp.int32, (2 * OWNERS, 2 * OWNERS), 0)
    at_column = lax.broadcasted_iota(jnp.int32, (2 * OWNERS, 2 * OWNERS), 1)
    places = jnp.where(at_row < OWNERS, 2 * at_row, 2 * at_row - 2 * OWNERS + 1)
    order = jnp.where(at_column == places, 1.0, 0.0).astype(jnp.bfloat16)
    high = value.astype(jnp.bfloat16)
    middle, low = halves(value - high.astype(jnp.float32))
    return dot(high, order) + (dot(middle, order) + dot(low, order))


def finish(*refs):
    count = len(refs) // 2
    copies = [
        pltpu.make_async_copy(refs[place], refs[count + place], refs[-1].at[place])
        for place in range(count)
    ]
    for copy in copies:
        copy.start()
    for copy in copies:
        copy.wait()


def keep(value):
    return pltpu.with_memory_space_constraint(value, pltpu.VMEM)


def per_device(tables, inputs, out_grad, readout, log_step, decay_log, rotation):
    norm_scale = 1.0 / math.sqrt(LENGTH)
    dma = pltpu.SemaphoreType.DMA
    any_space = pl.BlockSpec(memory_space=pl.ANY)
    vmem = pl.BlockSpec(memory_space=pltpu.VMEM)
    f32 = jnp.float32
    results = pl.pallas_call(
        functools.partial(kernel, norm_scale),
        out_shape=(
            pltpu.VMEM((OWNERS, 2, WIDTH), f32),
            pltpu.VMEM((2, STATES, 2 * OWNERS), f32),
            pltpu.VMEM((2, WIDTH), f32),
            pltpu.VMEM((2, STATES), f32),
        ),
        in_specs=[any_space] * 11,
        out_specs=(vmem,) * 4,
        scratch_shapes=[
            pltpu.VMEM((2, OWNERS, 2, WIDTH), jnp.bfloat16),
            pltpu.VMEM((2, OWNERS, 2, WIDTH), jnp.bfloat16),
            pltpu.VMEM((OWNERS, 2, WIDTH), f32),
            pltpu.VMEM((2, 1, WIDTH), f32),
            pltpu.VMEM((2, 8, 8, 2, 1, WIDTH), f32),
            pltpu.VMEM((2 * OWNERS, WIDTH), f32),
            pltpu.VMEM((1, WIDTH), f32),
            pltpu.VMEM((4, 8, 1, WIDTH), f32),
            pltpu.VMEM((2, WIDTH), f32),
            pltpu.VMEM((8, 2, WIDTH), f32),
            pltpu.VMEM((4, WIDTH), f32),
            pltpu.VMEM((16, 4, WIDTH), f32),
        ]
        + [
            pltpu.VMEM((2, STATES, 2 * OWNERS), f32),
            pltpu.SMEM((2 * OWNERS,), f32),
            pltpu.VMEM((1, STATES), f32),
            pltpu.VMEM((1, STATES), f32),
        ]
        + [pltpu.VMEM(table.shape, table.dtype) for table in tables]
        + [dma((2,)), dma((9,)), dma((2,)), dma((9,)), dma, dma, dma((4,)), dma, dma, dma],
        compiler_params=pltpu.CompilerParams(collective_id=0, has_side_effects=True),
        name="channel_rows",
    )(
        inputs.reshape(OWNERS, 2, WIDTH),
        out_grad.reshape(OWNERS, 2, WIDTH),
        jnp.transpose(readout, (0, 2, 1)),
        log_step,
        decay_log.reshape(1, STATES),
        rotation.reshape(1, STATES),
        *[jnp.asarray(table) for table in tables],
    )
    kernel_grad, readout_grad, step_grad, state_grad = pl.pallas_call(
        finish,
        out_shape=(
            jax.ShapeDtypeStruct((2 * OWNERS, WIDTH), f32),
            jax.ShapeDtypeStruct((2, STATES, 2 * OWNERS), f32),
            jax.ShapeDtypeStruct((2, WIDTH), f32),
            jax.ShapeDtypeStruct((2, STATES), f32),
        ),
        in_specs=[vmem] * 4,
        out_specs=(any_space,) * 4,
        scratch_shapes=[dma((4,))],
        name="finish",
    )(*[keep(value) for value in (results[0].reshape(2 * OWNERS, WIDTH), *results[1:])])
    return (
        kernel_grad,
        jnp.transpose(readout_grad, (0, 2, 1)),
        step_grad.reshape(2 * OWNERS),
        state_grad,
    )


def solution(mesh):
    tables = transform_tables()
    return jax.shard_map(
        functools.partial(per_device, tables),
        mesh=mesh,
        in_specs=(P("ch", "seq"), P("ch", "seq"), P(None, "ch", None), P("ch"), P(), P()),
        out_specs=(P("ch", "seq"), P(None, "ch", None), P("ch"), P()),
        check_vma=False,
    )
```

```python
import functools
import math

import jax
import jax.numpy as jnp
import numpy as np
from jax import lax
from jax.experimental import pallas as pl
from jax.experimental.pallas import tpu as pltpu
from jax.sharding import PartitionSpec as P

MESH = pl.DeviceIdType.MESH
OWNERS = 128
FIRST_ROW = 0
FIRST = 1
WIDTH = 128
LENGTH = OWNERS * WIDTH
STATES = 64


def split_table(table):
    high = np.asarray(table, np.float32).astype(jnp.bfloat16)
    low = (np.asarray(table, np.float64) - high.astype(np.float64)).astype(jnp.bfloat16)
    return np.stack([high, low])


def transform_tables():
    index = np.arange(WIDTH, dtype=np.float64)
    quarter = index + 0.25
    enter = 2.0 * np.pi * np.outer(quarter, index) / WIDTH
    spread = np.zeros((2, 2, WIDTH, OWNERS, 2))
    for channel in range(2):
        spread[0, channel, :, :, channel] = np.cos(enter)
        spread[1, channel, :, :, channel] = -np.sin(enter)
    first = spread.reshape(4 * WIDTH, 2 * OWNERS)
    turn = 2.0 * np.pi * np.outer(quarter, index) / LENGTH
    turns = np.stack([np.cos(turn), np.sin(turn)]).astype(np.float32)
    plain = 2.0 * np.pi * np.outer(index, index) / WIDTH
    cosine, sine = np.cos(plain), np.sin(plain)
    second = np.block([[cosine, -sine], [sine, cosine]])
    third = np.block([[cosine, sine], [-sine, cosine]])
    scale = 1.0 / (LENGTH * math.sqrt(LENGTH))
    leave = enter.T
    fourth = np.concatenate([np.cos(leave), -np.sin(leave)], axis=1) * scale
    return (
        split_table(first),
        turns,
        split_table(second),
        split_table(third),
        split_table(fourth),
    )


def dot(left, right):
    return jnp.dot(left, right, preferred_element_type=jnp.float32)


def halves(value):
    high = value.astype(jnp.bfloat16)
    return high, (value - high.astype(jnp.float32)).astype(jnp.bfloat16)


def dot_pair(left, right):
    return dot(left[0], right[0]) + (dot(left[0], right[1]) + dot(left[1], right[0]))


def sine_cosine(angle):
    turns = jnp.floor(angle * (2.0 / math.pi) + 0.5)
    rest = angle - turns * 1.5625
    rest = rest - turns * 0.0081787109375
    rest = rest - turns * 0.000116348266601562
    rest = rest - turns * 1.26759079665e-06
    square = rest * rest
    sine = rest + rest * square * (
        -1.6666667e-1 + square * (8.3333310e-3 + square * (-1.9840874e-4 + square * 2.7525562e-6))
    )
    cosine = (
        1.0
        - 0.5 * square
        + square
        * square
        * (4.16666667e-2 + square * (-1.38888889e-3 + square * (2.48015873e-5 - square * 2.7557319e-7)))
    )
    quadrant = turns - 4.0 * jnp.floor(turns * 0.25)
    odd = (quadrant == 1.0) | (quadrant == 3.0)
    sine_out = jnp.where(odd, cosine, sine)
    cosine_out = jnp.where(odd, sine, cosine)
    sine_out = jnp.where(quadrant >= 2.0, -sine_out, sine_out)
    cosine_out = jnp.where((quadrant == 1.0) | (quadrant == 2.0), -cosine_out, cosine_out)
    return sine_out, cosine_out


def exp_minus_one(value):
    series = 1.0 + value * (1.0 / 9.0)
    for count in (8.0, 7.0, 6.0, 5.0, 4.0, 3.0, 2.0):
        series = 1.0 + value * (1.0 / count) * series
    return jnp.where(jnp.abs(value) < 0.5, value * series, jnp.exp(value) - 1.0)


def multiply(left, right):
    return (left[0] * right[0] - left[1] * right[1], left[0] * right[1] + left[1] * right[0])


def conjugate(value):
    return (value[0], -value[1])


def primal_rows(step, decay, turn, readout):
    pole = (-jnp.exp(decay), turn)
    rate = (step * pole[0], step * pole[1])
    sine, cosine = sine_cosine(rate[1])
    half_sine, _ = sine_cosine(0.5 * rate[1])
    growth = jnp.exp(rate[0])
    lift = (
        exp_minus_one(rate[0]) * cosine - 2.0 * half_sine * half_sine,
        growth * sine,
    )
    norm = pole[0] * pole[0] + pole[1] * pole[1]
    inverse = (pole[0] / norm, -pole[1] / norm)
    ratio = multiply(lift, inverse)
    coef = multiply(readout, ratio)
    power = (growth * cosine, growth * sine)
    return dict(
        step=step, pole=pole, rate=rate, inverse=inverse, ratio=ratio, coef=coef, power=power
    )


def power_table(rate, positions):
    decays = jnp.exp(rate[0] * positions)
    sine, cosine = sine_cosine(rate[1] * positions)
    return decays * cosine, decays * sine


def correlate(signals, first, turns, second, third, fourth):
    spread = dot(first[0], signals) + dot(first[1], signals)
    turn_cos, turn_sin = turns[0], turns[1]
    blocks = []
    for channel in range(2):
        for signal in range(2):
            columns = slice(signal * WIDTH, (signal + 1) * WIDTH)
            real = spread[channel * WIDTH : (channel + 1) * WIDTH, columns]
            imag = spread[(2 + channel) * WIDTH : (3 + channel) * WIDTH, columns]
            blocks.append(
                jnp.concatenate(
                    [real * turn_cos + imag * turn_sin, imag * turn_cos - real * turn_sin], axis=1
                )
            )
    spectrum = dot_pair(halves(jnp.concatenate(blocks, axis=0)), second)
    products = []
    for channel in range(2):
        entry = spectrum[2 * channel * WIDTH : (2 * channel + 1) * WIDTH]
        exit_ = spectrum[(2 * channel + 1) * WIDTH : (2 * channel + 2) * WIDTH]
        in_real, in_imag = entry[:, :WIDTH], entry[:, WIDTH:]
        out_real, out_imag = exit_[:, :WIDTH], exit_[:, WIDTH:]
        products.append(
            jnp.concatenate(
                [
                    out_real * in_real + out_imag * in_imag,
                    out_imag * in_real - out_real * in_imag,
                ],
                axis=1,
            )
        )
    back = dot_pair(halves(jnp.concatenate(products, axis=0)), third)
    columns = []
    for channel in range(2):
        real = back[channel * WIDTH : (channel + 1) * WIDTH, :WIDTH]
        imag = back[channel * WIDTH : (channel + 1) * WIDTH, WIDTH:]
        columns.append(
            jnp.concatenate(
                [real * turn_cos - imag * turn_sin, real * turn_sin + imag * turn_cos], axis=0
            )
        )
    return dot_pair((fourth[0], fourth[1]), halves(jnp.concatenate(columns, axis=1)))


def sum_rows(value):
    return jnp.sum(value, axis=0, keepdims=True)


def power_sums(lags, tables, base, starts, norm_scale):
    stacked = jnp.concatenate([lags[:, :WIDTH], lags[:, WIDTH:]], axis=0)
    raw = dot_pair(halves(stacked), tables)
    lane = lax.broadcasted_iota(jnp.int32, (OWNERS, WIDTH), 1)
    picked = [
        jnp.where(
            lane < STATES,
            raw[:OWNERS, part * WIDTH : (part + 1) * WIDTH],
            raw[OWNERS:, part * WIDTH : (part + 1) * WIDTH],
        )
        for part in range(4)
    ]
    plain = (picked[0], picked[1])
    lagged = (starts * picked[0] + picked[2], starts * picked[1] + picked[3])
    powers = multiply(base, plain)
    lag_powers = multiply(base, lagged)
    return (
        (norm_scale * sum_rows(powers[0]), norm_scale * sum_rows(powers[1])),
        (norm_scale * sum_rows(lag_powers[0]), norm_scale * sum_rows(lag_powers[1])),
    )


def parameter_rows(primal, readout, powers, lag_powers):
    coef_grad = (2.0 * powers[0], -2.0 * powers[1])
    readout_grad = multiply(conjugate(primal["ratio"]), coef_grad)
    ratio_grad = multiply(conjugate(readout), coef_grad)
    shifted = multiply(primal["coef"], lag_powers)
    lift_grad = multiply(conjugate(primal["inverse"]), ratio_grad)
    through = multiply(conjugate(primal["power"]), lift_grad)
    rate_grad = (2.0 * shifted[0] + through[0], -2.0 * shifted[1] + through[1])
    direct = multiply(conjugate(primal["ratio"]), lift_grad)
    step, pole = primal["step"], primal["pole"]
    pole_grad = (step * rate_grad[0] - direct[0], step * rate_grad[1] - direct[1])
    step_terms = step * (rate_grad[0] * pole[0] + rate_grad[1] * pole[1])
    return readout_grad, step_terms, (pole_grad[0] * pole[0], pole_grad[1])


def offset_of(place, ring):
    return ring // 2 + (1 - 2 * (place % 2)) * ((place + 1) // 2)


def place_of(me):
    return me // 16, (me // 2) % 8, me % 2


def ring_places(place, ring):
    return [(place + offset_of(count, ring)) % ring for count in range(ring)]


def per_peer(me, action):
    y, z, core = place_of(me)
    to_y = [16 * other for other in ring_places(y, 8)]
    to_z = [2 * other for other in ring_places(z, 8)]
    to_core = [1 - core, core]
    peers = [at_y + at_z + at_core for at_y in to_y for at_z in to_z for at_core in to_core]
    for peer in peers[:-1]:
        action(peer)


def kernel(
    norm_scale,
    inputs_ref,
    grads_ref,
    readout_in,
    log_step_in,
    decay_in,
    rotation_in,
    first_ref,
    turns_ref,
    second_ref,
    third_ref,
    fourth_ref,
    lags_out,
    sorted_out,
    step_out,
    state_out,
    outgoing,
    arrived,
    lag_rows,
    readout_rows,
    readout_all,
    readout_turned,
    state_rows,
    state_in,
    step_rows,
    step_in,
    column_rows,
    column_in,
    column_step_rows,
    column_step_in,
    first_in,
    readout_ref,
    log_step_ref,
    decay_ref,
    rotation_ref,
    first,
    turns,
    second,
    third,
    fourth,
    stage_sem,
    table_sem,
    own_sem,
    send_sem,
    signal_sem,
    lag_sem,
    readout_sem,
    state_sem,
    step_sem,
    column_sem,
    column_step_sem,
    first_sem,
):
    me = lax.axis_index("seq")
    row = lax.axis_index("ch")
    y, z, core = place_of(me)
    is_first = jnp.logical_and(row == FIRST_ROW, me == FIRST)
    feeds_first = jnp.logical_and(row == FIRST_ROW, jnp.logical_and(y == 0, me != FIRST))
    stages = [
        pltpu.make_async_copy(inputs_ref, outgoing.at[0], stage_sem.at[0]),
        pltpu.make_async_copy(grads_ref, outgoing.at[1], stage_sem.at[1]),
    ]
    for copy in stages:
        copy.start()
    barrier = pltpu.get_barrier_semaphore()

    def greet(peer):
        pl.semaphore_signal(barrier, inc=1, device_id={"seq": peer}, device_id_type=MESH)

    per_peer(me, greet)
    around_y = ring_places(y, 8)
    around_z = ring_places(z, 8)
    around_x = [(row + step) % 4 for step in (2, 1, 3, 0)]
    across = [(at_x, 16 * at_y + 2 * z + core) for at_x in around_x[:3] for at_y in around_y]
    for at_x, peer in across:
        pl.semaphore_signal(
            barrier, inc=1, device_id={"ch": at_x, "seq": peer}, device_id_type=MESH
        )

    @pl.when(is_first)
    def _():
        for at_x in around_x[:3]:

            def hail(peer, carry, at_x=at_x):
                pl.semaphore_signal(
                    barrier, inc=1, device_id={"ch": at_x, "seq": peer}, device_id_type=MESH
                )
                return carry

            lax.fori_loop(0, OWNERS, hail, 0)

    loads = [
        pltpu.make_async_copy(source, target, table_sem.at[place])
        for place, (source, target) in enumerate(
            (
                (log_step_in, log_step_ref),
                (decay_in, decay_ref),
                (rotation_in, rotation_ref),
                (readout_in, readout_ref),
                (first_ref, first),
                (turns_ref, turns),
                (second_ref, second),
                (third_ref, third),
                (fourth_ref, fourth),
            )
        )
    ]
    for copy in loads:
        copy.start()
    for copy in stages:
        copy.wait()
    pl.semaphore_wait(barrier, OWNERS - 1 + len(across) + (row + 3) // 4)

    def send(source, target, sent, received, device):
        pltpu.make_async_remote_copy(
            src_ref=source,
            dst_ref=target,
            send_sem=sent,
            recv_sem=received,
            device_id=device,
            device_id_type=MESH,
        ).start()

    own = pltpu.make_async_copy(outgoing.at[:, me], arrived.at[:, me], own_sem.at[0])
    own.start()
    per_peer(
        me,
        lambda peer: send(
            outgoing.at[:, peer], arrived.at[:, me], send_sem.at[0], signal_sem, {"seq": peer}
        ),
    )

    for copy in loads[:4]:
        copy.wait()
    lane_row = lax.broadcasted_iota(jnp.int32, (1, WIDTH), 1)
    left = lane_row < STATES
    step_row = jnp.exp(jnp.where(left, log_step_ref[2 * me], log_step_ref[2 * me + 1]))
    decay_row = jnp.concatenate([decay_ref[...], decay_ref[...]], axis=1)
    turn_row = jnp.concatenate([rotation_ref[...], rotation_ref[...]], axis=1)
    readout_turned[...] = jnp.transpose(
        jnp.concatenate([readout_ref[0], readout_ref[1]], axis=0), (1, 0)
    )
    low = readout_turned[pl.ds(2 * me, 1), :]
    high = readout_turned[pl.ds(2 * me + 1, 1), :]
    readout = (
        jnp.where(left, low, pltpu.roll(high, STATES, 1)),
        jnp.where(left, pltpu.roll(low, STATES, 1), high),
    )
    primal = primal_rows(step_row, decay_row, turn_row, readout)
    offsets = lax.broadcasted_iota(jnp.int32, (WIDTH, WIDTH), 0).astype(jnp.float32)
    starts = offsets * float(WIDTH)
    near = power_table(primal["rate"], offsets)
    base = power_table(primal["rate"], starts)
    tables = halves(
        jnp.concatenate([near[0], near[1], offsets * near[0], offsets * near[1]], axis=1)
    )
    for copy in loads[4:]:
        copy.wait()

    own.wait()
    rest = arrived.at[:, pl.ds(0, OWNERS - 1)]
    pltpu.make_async_copy(rest, rest, signal_sem).wait()
    signals = jnp.concatenate(
        [arrived.reshape(2, 2 * OWNERS, WIDTH)[0], arrived.reshape(2, 2 * OWNERS, WIDTH)[1]],
        axis=1,
    )
    lags = correlate(signals, first, turns, second, third, fourth)
    lag_rows[:, 0, :] = lags[:, :WIDTH]
    lag_rows[:, 1, :] = lags[:, WIDTH:]

    powers, lag_powers = power_sums(lags, tables, base, starts, norm_scale)
    readout_grad, step_terms, state_grad = parameter_rows(primal, readout, powers, lag_powers)
    state_rows[...] = jnp.where(
        left,
        state_grad[0] + pltpu.roll(state_grad[0], STATES, 1),
        state_grad[1] + pltpu.roll(state_grad[1], STATES, 1),
    )
    line = [16 * at_y + 2 * z + core for at_y in around_y[:-1]]

    @pl.when(jnp.logical_not(is_first))
    def _():
        send(
            state_rows,
            first_in.at[2 * z + core, 8 * row + y],
            send_sem.at[9],
            first_sem,
            {"ch": jnp.int32(FIRST_ROW), "seq": jnp.int32(FIRST)},
        )

    for at_x, peer in across + [(around_x[3], peer) for peer in line]:
        send(
            state_rows,
            state_in.at[row, y],
            send_sem.at[3],
            state_sem,
            {"ch": at_x, "seq": peer},
        )
    state_in[row, y] = state_rows[...]

    @pl.when(is_first)
    def _():
        first_in[FIRST, 0] = state_rows[...]

    first_step = jnp.sum(jnp.where(left, step_terms, 0.0), axis=1, keepdims=True)
    second_step = jnp.sum(jnp.where(left, 0.0, step_terms), axis=1, keepdims=True)
    count = WIDTH * lax.broadcasted_iota(jnp.int32, (2, WIDTH), 0) + lax.broadcasted_iota(
        jnp.int32, (2, WIDTH), 1
    )
    step_rows[...] = jnp.where(
        count == 2 * me, first_step, jnp.where(count == 2 * me + 1, second_step, 0.0)
    )
    step_in[y] = step_rows[...]
    readout_rows[0] = readout_grad[0]
    readout_rows[1] = readout_grad[1]
    readout_all[0, y, z, core] = readout_grad[0]
    readout_all[1, y, z, core] = readout_grad[1]
    for peer in line:
        send(
            readout_rows.at[0],
            readout_all.at[0, y, z, core],
            send_sem.at[2],
            readout_sem.at[0],
            {"seq": peer},
        )
    for at_z in around_z[:-1]:
        send(
            readout_rows.at[1],
            readout_all.at[1, y, z, core],
            send_sem.at[6],
            readout_sem.at[1],
            {"seq": 16 * y + 2 * at_z + core},
        )
    for peer in line:
        send(step_rows, step_in.at[y], send_sem.at[4], step_sem, {"seq": peer})
    own_lags = pltpu.make_async_copy(lag_rows.at[me], lags_out.at[me], own_sem.at[1])
    own_lags.start()
    per_peer(
        me,
        lambda peer: send(
            lag_rows.at[peer], lags_out.at[me], send_sem.at[1], lag_sem, {"seq": peer}
        ),
    )

    def await_bytes(part, *semaphores):
        for semaphore in semaphores:
            pltpu.make_async_copy(part, part, semaphore).wait()

    ends = [16 * at_y + 2 * z + at_core for at_y in around_y for at_core in (1 - core, core)]
    column = [16 * y + 2 * at_z + at_core for at_z in around_z for at_core in (1 - core, core)]
    real_line = readout_all.at[0, :, z, core]
    imag_line = readout_all.at[1, y, :, core]
    seven = readout_all.at[0, pl.ds(0, 7), 0, 0]
    await_bytes(seven, readout_sem.at[0])
    for peer in column[:-1]:
        send(real_line, real_line, send_sem.at[7], readout_sem.at[2], {"seq": peer})
    await_bytes(seven, readout_sem.at[1])
    for peer in ends[:-1]:
        send(imag_line, imag_line, send_sem.at[8], readout_sem.at[3], {"seq": peer})

    most = state_in.reshape(32, 1, WIDTH).at[pl.ds(0, 31)]
    await_bytes(step_in.at[pl.ds(0, 7)], step_sem)
    column_step_rows[...] = sum_in_order(step_in, 8)
    column_step_in[2 * z + core] = column_step_rows[...]
    for peer in column[:-1]:
        send(
            column_step_rows,
            column_step_in.at[2 * z + core],
            send_sem.at[10],
            column_step_sem,
            {"seq": peer},
        )
    await_bytes(most, state_sem)
    column_rows[...] = sum_rows(state_in.reshape(32, WIDTH)[...])
    column_in[2 * z + core] = column_rows[...]
    for peer in column[:-1]:

        @pl.when(jnp.logical_or(row != FIRST_ROW, peer != FIRST))
        def _(peer=peer):
            send(
                column_rows, column_in.at[2 * z + core], send_sem.at[5], column_sem, {"seq": peer}
            )

    fifteen = readout_all.at[0].reshape(16, 8, 1, WIDTH).at[pl.ds(0, 15)]
    await_bytes(fifteen, readout_sem.at[2], readout_sem.at[3])
    sorted_ = sort_channels(readout_all.reshape(2, OWNERS, WIDTH))
    sorted_out[0] = sorted_[:STATES]
    sorted_out[1] = sorted_[STATES:]
    own_lags.wait()
    part = lags_out.at[pl.ds(0, OWNERS - 1)]
    await_bytes(part, lag_sem, send_sem.at[1])
    await_bytes(fifteen, send_sem.at[7], send_sem.at[8])
    await_bytes(seven, send_sem.at[2], send_sem.at[6])
    await_bytes(rest, send_sem.at[0])
    await_bytes(most, send_sem.at[3])
    await_bytes(step_in.at[pl.ds(0, 7)], send_sem.at[4])
    step_ended = column_step_in.at[pl.ds(0, 15)]
    await_bytes(step_ended, column_step_sem, send_sem.at[10])
    step_out[...] = sum_in_order(column_step_in, 16)
    await_bytes(column_in.at[pl.ds(0, 14)], send_sem.at[5])

    def put_state(state):
        state_out[0:1, :] = state[:, :STATES]
        state_out[1:2, :] = state[:, STATES:]

    @pl.when(jnp.logical_not(feeds_first))
    def _():
        await_bytes(column_in.at[pl.ds(0, 1)], send_sem.at[5])

    @pl.when(is_first)
    def _():
        await_bytes(first_in.reshape(512, 1, WIDTH).at[pl.ds(0, 511)], first_sem)
        every = first_in.reshape(16, 32, WIDTH)
        put_state(sum_in_order([sum_rows(every[place]) for place in range(16)], 16))

    @pl.when(jnp.logical_not(is_first))
    def _():
        await_bytes(column_in.at[pl.ds(0, 1)], send_sem.at[9])
        await_bytes(column_in.at[pl.ds(0, 15)], column_sem)
        put_state(sum_in_order(column_in, 16))


def sum_in_order(buffer, count):
    parts = [buffer[place] for place in range(count)]
    while len(parts) > 1:
        parts = [parts[place] + parts[place + 1] for place in range(0, len(parts), 2)]
    return parts[0]


def sort_channels(rows_ref):
    blocks = []
    for part in range(2):
        turned = jnp.transpose(rows_ref[part], (1, 0))
        blocks.append(jnp.concatenate([turned[:STATES], turned[STATES:]], axis=1))
    value = jnp.concatenate(blocks, axis=0)
    at_row = lax.broadcasted_iota(jnp.int32, (2 * OWNERS, 2 * OWNERS), 0)
    at_column = lax.broadcasted_iota(jnp.int32, (2 * OWNERS, 2 * OWNERS), 1)
    places = jnp.where(at_row < OWNERS, 2 * at_row, 2 * at_row - 2 * OWNERS + 1)
    order = jnp.where(at_column == places, 1.0, 0.0).astype(jnp.bfloat16)
    high = value.astype(jnp.bfloat16)
    middle, low = halves(value - high.astype(jnp.float32))
    return dot(high, order) + (dot(middle, order) + dot(low, order))


def finish(*refs):
    count = len(refs) // 2
    copies = [
        pltpu.make_async_copy(refs[place], refs[count + place], refs[-1].at[place])
        for place in range(count)
    ]
    for copy in copies:
        copy.start()
    for copy in copies:
        copy.wait()


def keep(value):
    return pltpu.with_memory_space_constraint(value, pltpu.VMEM)


def per_device(tables, inputs, out_grad, readout, log_step, decay_log, rotation):
    norm_scale = 1.0 / math.sqrt(LENGTH)
    dma = pltpu.SemaphoreType.DMA
    any_space = pl.BlockSpec(memory_space=pl.ANY)
    vmem = pl.BlockSpec(memory_space=pltpu.VMEM)
    f32 = jnp.float32
    results = pl.pallas_call(
        functools.partial(kernel, norm_scale),
        out_shape=(
            pltpu.VMEM((OWNERS, 2, WIDTH), f32),
            pltpu.VMEM((2, STATES, 2 * OWNERS), f32),
            pltpu.VMEM((2, WIDTH), f32),
            pltpu.VMEM((2, STATES), f32),
        ),
        in_specs=[any_space] * 11,
        out_specs=(vmem,) * 4,
        scratch_shapes=[
            pltpu.VMEM((2, OWNERS, 2, WIDTH), jnp.bfloat16),
            pltpu.VMEM((2, OWNERS, 2, WIDTH), jnp.bfloat16),
            pltpu.VMEM((OWNERS, 2, WIDTH), f32),
            pltpu.VMEM((2, 1, WIDTH), f32),
            pltpu.VMEM((2, 8, 8, 2, 1, WIDTH), f32),
            pltpu.VMEM((2 * OWNERS, WIDTH), f32),
            pltpu.VMEM((1, WIDTH), f32),
            pltpu.VMEM((4, 8, 1, WIDTH), f32),
            pltpu.VMEM((2, WIDTH), f32),
            pltpu.VMEM((8, 2, WIDTH), f32),
            pltpu.VMEM((1, WIDTH), f32),
            pltpu.VMEM((16, 1, WIDTH), f32),
            pltpu.VMEM((2, WIDTH), f32),
            pltpu.VMEM((16, 2, WIDTH), f32),
            pltpu.VMEM((16, 32, 1, WIDTH), f32),
        ]
        + [
            pltpu.VMEM((2, STATES, 2 * OWNERS), f32),
            pltpu.SMEM((2 * OWNERS,), f32),
            pltpu.VMEM((1, STATES), f32),
            pltpu.VMEM((1, STATES), f32),
        ]
        + [pltpu.VMEM(table.shape, table.dtype) for table in tables]
        + [dma((2,)), dma((9,)), dma((2,)), dma((11,)), dma, dma, dma((4,)), dma, dma, dma, dma, dma],
        compiler_params=pltpu.CompilerParams(collective_id=0, has_side_effects=True),
        name="channel_rows",
    )(
        inputs.reshape(OWNERS, 2, WIDTH),
        out_grad.reshape(OWNERS, 2, WIDTH),
        jnp.transpose(readout, (0, 2, 1)),
        log_step,
        decay_log.reshape(1, STATES),
        rotation.reshape(1, STATES),
        *[jnp.asarray(table) for table in tables],
    )
    kernel_grad, readout_grad, step_grad, state_grad = pl.pallas_call(
        finish,
        out_shape=(
            jax.ShapeDtypeStruct((2 * OWNERS, WIDTH), f32),
            jax.ShapeDtypeStruct((2, STATES, 2 * OWNERS), f32),
            jax.ShapeDtypeStruct((2, WIDTH), f32),
            jax.ShapeDtypeStruct((2, STATES), f32),
        ),
        in_specs=[vmem] * 4,
        out_specs=(any_space,) * 4,
        scratch_shapes=[dma((4,))],
        name="finish",
    )(*[keep(value) for value in (results[0].reshape(2 * OWNERS, WIDTH), *results[1:])])
    return (
        kernel_grad,
        jnp.transpose(readout_grad, (0, 2, 1)),
        step_grad.reshape(2 * OWNERS),
        state_grad,
    )


def solution(mesh):
    tables = transform_tables()
    return jax.shard_map(
        functools.partial(per_device, tables),
        mesh=mesh,
        in_specs=(P("ch", "seq"), P("ch", "seq"), P(None, "ch", None), P("ch"), P(), P()),
        out_specs=(P("ch", "seq"), P(None, "ch", None), P("ch"), P()),
        check_vma=False,
    )
```

```python
import functools
import math

import jax
import jax.numpy as jnp
import numpy as np
from jax import lax
from jax.experimental import pallas as pl
from jax.experimental.pallas import tpu as pltpu
from jax.sharding import PartitionSpec as P

MESH = pl.DeviceIdType.MESH
OWNERS = 128
WIDTH = 128
LENGTH = OWNERS * WIDTH
STATES = 64


def split_table(table):
    high = np.asarray(table, np.float32).astype(jnp.bfloat16)
    low = (np.asarray(table, np.float64) - high.astype(np.float64)).astype(jnp.bfloat16)
    return np.stack([high, low])


def transform_tables():
    index = np.arange(WIDTH, dtype=np.float64)
    quarter = index + 0.25
    enter = 2.0 * np.pi * np.outer(quarter, index) / WIDTH
    spread = np.zeros((2, 2, WIDTH, OWNERS, 2))
    for channel in range(2):
        spread[0, channel, :, :, channel] = np.cos(enter)
        spread[1, channel, :, :, channel] = -np.sin(enter)
    first = spread.reshape(4 * WIDTH, 2 * OWNERS)
    turn = 2.0 * np.pi * np.outer(quarter, index) / LENGTH
    turns = np.stack([np.cos(turn), np.sin(turn)]).astype(np.float32)
    plain = 2.0 * np.pi * np.outer(index, index) / WIDTH
    cosine, sine = np.cos(plain), np.sin(plain)
    second = np.block([[cosine, -sine], [sine, cosine]])
    third = np.block([[cosine, sine], [-sine, cosine]])
    scale = 1.0 / (LENGTH * math.sqrt(LENGTH))
    leave = enter.T
    fourth = np.concatenate([np.cos(leave), -np.sin(leave)], axis=1) * scale
    return (
        split_table(first),
        turns,
        split_table(second),
        split_table(third),
        split_table(fourth),
    )


def dot(left, right):
    return jnp.dot(left, right, preferred_element_type=jnp.float32)


def halves(value):
    high = value.astype(jnp.bfloat16)
    return high, (value - high.astype(jnp.float32)).astype(jnp.bfloat16)


def dot_pair(left, right):
    return dot(left[0], right[0]) + (dot(left[0], right[1]) + dot(left[1], right[0]))


def sine_cosine(angle):
    turns = jnp.floor(angle * (2.0 / math.pi) + 0.5)
    rest = angle - turns * 1.5625
    rest = rest - turns * 0.0081787109375
    rest = rest - turns * 0.000116348266601562
    rest = rest - turns * 1.26759079665e-06
    square = rest * rest
    sine = rest + rest * square * (
        -1.6666667e-1 + square * (8.3333310e-3 + square * (-1.9840874e-4 + square * 2.7525562e-6))
    )
    cosine = (
        1.0
        - 0.5 * square
        + square
        * square
        * (4.16666667e-2 + square * (-1.38888889e-3 + square * (2.48015873e-5 - square * 2.7557319e-7)))
    )
    quadrant = turns - 4.0 * jnp.floor(turns * 0.25)
    odd = (quadrant == 1.0) | (quadrant == 3.0)
    sine_out = jnp.where(odd, cosine, sine)
    cosine_out = jnp.where(odd, sine, cosine)
    sine_out = jnp.where(quadrant >= 2.0, -sine_out, sine_out)
    cosine_out = jnp.where((quadrant == 1.0) | (quadrant == 2.0), -cosine_out, cosine_out)
    return sine_out, cosine_out


def exp_minus_one(value):
    series = 1.0 + value * (1.0 / 9.0)
    for count in (8.0, 7.0, 6.0, 5.0, 4.0, 3.0, 2.0):
        series = 1.0 + value * (1.0 / count) * series
    return jnp.where(jnp.abs(value) < 0.5, value * series, jnp.exp(value) - 1.0)


def multiply(left, right):
    return (left[0] * right[0] - left[1] * right[1], left[0] * right[1] + left[1] * right[0])


def conjugate(value):
    return (value[0], -value[1])


def primal_rows(step, decay, turn, readout):
    pole = (-jnp.exp(decay), turn)
    rate = (step * pole[0], step * pole[1])
    sine, cosine = sine_cosine(rate[1])
    half_sine, _ = sine_cosine(0.5 * rate[1])
    growth = jnp.exp(rate[0])
    lift = (
        exp_minus_one(rate[0]) * cosine - 2.0 * half_sine * half_sine,
        growth * sine,
    )
    norm = pole[0] * pole[0] + pole[1] * pole[1]
    inverse = (pole[0] / norm, -pole[1] / norm)
    ratio = multiply(lift, inverse)
    coef = multiply(readout, ratio)
    power = (growth * cosine, growth * sine)
    return dict(
        step=step, pole=pole, rate=rate, inverse=inverse, ratio=ratio, coef=coef, power=power
    )


def power_table(rate, positions):
    decays = jnp.exp(rate[0] * positions)
    sine, cosine = sine_cosine(rate[1] * positions)
    return decays * cosine, decays * sine


def correlate(signals, first, turns, second, third, fourth):
    spread = dot(first[0], signals) + dot(first[1], signals)
    turn_cos, turn_sin = turns[0], turns[1]
    blocks = []
    for channel in range(2):
        for signal in range(2):
            columns = slice(signal * WIDTH, (signal + 1) * WIDTH)
            real = spread[channel * WIDTH : (channel + 1) * WIDTH, columns]
            imag = spread[(2 + channel) * WIDTH : (3 + channel) * WIDTH, columns]
            blocks.append(
                jnp.concatenate(
                    [real * turn_cos + imag * turn_sin, imag * turn_cos - real * turn_sin], axis=1
                )
            )
    spectrum = dot_pair(halves(jnp.concatenate(blocks, axis=0)), second)
    products = []
    for channel in range(2):
        entry = spectrum[2 * channel * WIDTH : (2 * channel + 1) * WIDTH]
        exit_ = spectrum[(2 * channel + 1) * WIDTH : (2 * channel + 2) * WIDTH]
        in_real, in_imag = entry[:, :WIDTH], entry[:, WIDTH:]
        out_real, out_imag = exit_[:, :WIDTH], exit_[:, WIDTH:]
        products.append(
            jnp.concatenate(
                [
                    out_real * in_real + out_imag * in_imag,
                    out_imag * in_real - out_real * in_imag,
                ],
                axis=1,
            )
        )
    back = dot_pair(halves(jnp.concatenate(products, axis=0)), third)
    columns = []
    for channel in range(2):
        real = back[channel * WIDTH : (channel + 1) * WIDTH, :WIDTH]
        imag = back[channel * WIDTH : (channel + 1) * WIDTH, WIDTH:]
        columns.append(
            jnp.concatenate(
                [real * turn_cos - imag * turn_sin, real * turn_sin + imag * turn_cos], axis=0
            )
        )
    return dot_pair((fourth[0], fourth[1]), halves(jnp.concatenate(columns, axis=1)))


def sum_rows(value):
    return jnp.sum(value, axis=0, keepdims=True)


def power_sums(lags, tables, base, starts, norm_scale):
    stacked = jnp.concatenate([lags[:, :WIDTH], lags[:, WIDTH:]], axis=0)
    raw = dot_pair(halves(stacked), tables)
    lane = lax.broadcasted_iota(jnp.int32, (OWNERS, WIDTH), 1)
    picked = [
        jnp.where(
            lane < STATES,
            raw[:OWNERS, part * WIDTH : (part + 1) * WIDTH],
            raw[OWNERS:, part * WIDTH : (part + 1) * WIDTH],
        )
        for part in range(4)
    ]
    plain = (picked[0], picked[1])
    lagged = (starts * picked[0] + picked[2], starts * picked[1] + picked[3])
    powers = multiply(base, plain)
    lag_powers = multiply(base, lagged)
    return (
        (norm_scale * sum_rows(powers[0]), norm_scale * sum_rows(powers[1])),
        (norm_scale * sum_rows(lag_powers[0]), norm_scale * sum_rows(lag_powers[1])),
    )


def parameter_rows(primal, readout, powers, lag_powers):
    coef_grad = (2.0 * powers[0], -2.0 * powers[1])
    readout_grad = multiply(conjugate(primal["ratio"]), coef_grad)
    ratio_grad = multiply(conjugate(readout), coef_grad)
    shifted = multiply(primal["coef"], lag_powers)
    lift_grad = multiply(conjugate(primal["inverse"]), ratio_grad)
    through = multiply(conjugate(primal["power"]), lift_grad)
    rate_grad = (2.0 * shifted[0] + through[0], -2.0 * shifted[1] + through[1])
    direct = multiply(conjugate(primal["ratio"]), lift_grad)
    step, pole = primal["step"], primal["pole"]
    pole_grad = (step * rate_grad[0] - direct[0], step * rate_grad[1] - direct[1])
    step_terms = step * (rate_grad[0] * pole[0] + rate_grad[1] * pole[1])
    return readout_grad, step_terms, (pole_grad[0] * pole[0], pole_grad[1])


def offset_of(place, ring):
    return ring // 2 + (1 - 2 * (place % 2)) * ((place + 1) // 2)


def place_of(me):
    return me // 16, (me // 2) % 8, me % 2


def ring_places(place, ring):
    return [(place + offset_of(count, ring)) % ring for count in range(ring)]


def hop_order():
    draws = np.random.RandomState(0).permutation(OWNERS)
    offsets = [(at // 16, at // 2 % 8, at % 2) for at in range(1, OWNERS)]
    hops = [min(y, 8 - y) + min(z, 8 - z) for y, z, _ in offsets]
    places = sorted(range(OWNERS - 1), key=lambda at: (-hops[at], draws[at]))
    return [offsets[at] for at in places]


def per_peer(me, action):
    y, z, core = place_of(me)
    to_y = [16 * ((y + step) % 8) for step in range(8)]
    to_z = [2 * ((z + step) % 8) for step in range(8)]
    to_core = [core, 1 - core]
    for step_y, step_z, step_core in hop_order():
        action(to_y[step_y] + to_z[step_z] + to_core[step_core])


def kernel(
    norm_scale,
    inputs_ref,
    grads_ref,
    readout_in,
    log_step_in,
    decay_in,
    rotation_in,
    first_ref,
    turns_ref,
    second_ref,
    third_ref,
    fourth_ref,
    lags_out,
    sorted_out,
    step_out,
    state_out,
    outgoing,
    arrived,
    lag_rows,
    readout_rows,
    readout_all,
    readout_turned,
    state_rows,
    state_in,
    step_rows,
    step_in,
    column_rows,
    column_in,
    readout_ref,
    log_step_ref,
    decay_ref,
    rotation_ref,
    first,
    turns,
    second,
    third,
    fourth,
    stage_sem,
    table_sem,
    own_sem,
    send_sem,
    signal_sem,
    lag_sem,
    readout_sem,
    state_sem,
    step_sem,
    column_sem,
):
    me = lax.axis_index("seq")
    row = lax.axis_index("ch")
    y, z, core = place_of(me)
    stages = [
        pltpu.make_async_copy(inputs_ref, outgoing.at[0], stage_sem.at[0]),
        pltpu.make_async_copy(grads_ref, outgoing.at[1], stage_sem.at[1]),
    ]
    for copy in stages:
        copy.start()
    barrier = pltpu.get_barrier_semaphore()

    def greet(peer):
        pl.semaphore_signal(barrier, inc=1, device_id={"seq": peer}, device_id_type=MESH)

    per_peer(me, greet)
    around_y = ring_places(y, 8)
    around_z = ring_places(z, 8)
    around_x = [(row + step) % 4 for step in (2, 1, 3, 0)]
    across = [(at_x, 16 * at_y + 2 * z + core) for at_x in around_x[:3] for at_y in around_y]
    for at_x, peer in across:
        pl.semaphore_signal(
            barrier, inc=1, device_id={"ch": at_x, "seq": peer}, device_id_type=MESH
        )
    loads = [
        pltpu.make_async_copy(source, target, table_sem.at[place])
        for place, (source, target) in enumerate(
            (
                (log_step_in, log_step_ref),
                (decay_in, decay_ref),
                (rotation_in, rotation_ref),
                (readout_in, readout_ref),
                (first_ref, first),
                (turns_ref, turns),
                (second_ref, second),
                (third_ref, third),
                (fourth_ref, fourth),
            )
        )
    ]
    for copy in loads:
        copy.start()
    for copy in stages:
        copy.wait()
    pl.semaphore_wait(barrier, OWNERS - 1 + len(across))

    def send(source, target, sent, received, device):
        pltpu.make_async_remote_copy(
            src_ref=source,
            dst_ref=target,
            send_sem=sent,
            recv_sem=received,
            device_id=device,
            device_id_type=MESH,
        ).start()

    own = pltpu.make_async_copy(outgoing.at[:, me], arrived.at[:, me], own_sem.at[0])
    own.start()
    per_peer(
        me,
        lambda peer: send(
            outgoing.at[:, peer], arrived.at[:, me], send_sem.at[0], signal_sem, {"seq": peer}
        ),
    )

    for copy in loads[:4]:
        copy.wait()
    lane_row = lax.broadcasted_iota(jnp.int32, (1, WIDTH), 1)
    left = lane_row < STATES
    step_row = jnp.exp(jnp.where(left, log_step_ref[2 * me], log_step_ref[2 * me + 1]))
    decay_row = jnp.concatenate([decay_ref[...], decay_ref[...]], axis=1)
    turn_row = jnp.concatenate([rotation_ref[...], rotation_ref[...]], axis=1)
    readout_turned[...] = jnp.transpose(
        jnp.concatenate([readout_ref[0], readout_ref[1]], axis=0), (1, 0)
    )
    low = readout_turned[pl.ds(2 * me, 1), :]
    high = readout_turned[pl.ds(2 * me + 1, 1), :]
    readout = (
        jnp.where(left, low, pltpu.roll(high, STATES, 1)),
        jnp.where(left, pltpu.roll(low, STATES, 1), high),
    )
    primal = primal_rows(step_row, decay_row, turn_row, readout)
    offsets = lax.broadcasted_iota(jnp.int32, (WIDTH, WIDTH), 0).astype(jnp.float32)
    starts = offsets * float(WIDTH)
    near = power_table(primal["rate"], offsets)
    base = power_table(primal["rate"], starts)
    tables = halves(
        jnp.concatenate([near[0], near[1], offsets * near[0], offsets * near[1]], axis=1)
    )
    for copy in loads[4:]:
        copy.wait()

    own.wait()
    rest = arrived.at[:, pl.ds(0, OWNERS - 1)]
    pltpu.make_async_copy(rest, rest, signal_sem).wait()
    signals = jnp.concatenate(
        [arrived.reshape(2, 2 * OWNERS, WIDTH)[0], arrived.reshape(2, 2 * OWNERS, WIDTH)[1]],
        axis=1,
    )
    lags = correlate(signals, first, turns, second, third, fourth)
    lag_rows[:, 0, :] = lags[:, :WIDTH]
    lag_rows[:, 1, :] = lags[:, WIDTH:]

    powers, lag_powers = power_sums(lags, tables, base, starts, norm_scale)
    readout_grad, step_terms, state_grad = parameter_rows(primal, readout, powers, lag_powers)
    state_rows[...] = jnp.where(
        left,
        state_grad[0] + pltpu.roll(state_grad[0], STATES, 1),
        state_grad[1] + pltpu.roll(state_grad[1], STATES, 1),
    )
    line = [16 * at_y + 2 * z + core for at_y in around_y[:-1]]
    for at_x, peer in across + [(around_x[3], peer) for peer in line]:
        send(
            state_rows,
            state_in.at[row, y],
            send_sem.at[3],
            state_sem,
            {"ch": at_x, "seq": peer},
        )
    state_in[row, y] = state_rows[...]
    first_step = jnp.sum(jnp.where(left, step_terms, 0.0), axis=1, keepdims=True)
    second_step = jnp.sum(jnp.where(left, 0.0, step_terms), axis=1, keepdims=True)
    count = WIDTH * lax.broadcasted_iota(jnp.int32, (2, WIDTH), 0) + lax.broadcasted_iota(
        jnp.int32, (2, WIDTH), 1
    )
    step_rows[...] = jnp.where(
        count == 2 * me, first_step, jnp.where(count == 2 * me + 1, second_step, 0.0)
    )
    step_in[y] = step_rows[...]
    readout_rows[0] = readout_grad[0]
    readout_rows[1] = readout_grad[1]
    readout_all[0, y, z, core] = readout_grad[0]
    readout_all[1, y, z, core] = readout_grad[1]
    for peer in line:
        send(
            readout_rows.at[0],
            readout_all.at[0, y, z, core],
            send_sem.at[2],
            readout_sem.at[0],
            {"seq": peer},
        )
    for at_z in around_z[:-1]:
        send(
            readout_rows.at[1],
            readout_all.at[1, y, z, core],
            send_sem.at[6],
            readout_sem.at[1],
            {"seq": 16 * y + 2 * at_z + core},
        )
    for peer in line:
        send(step_rows, step_in.at[y], send_sem.at[4], step_sem, {"seq": peer})
    own_lags = pltpu.make_async_copy(lag_rows.at[me], lags_out.at[me], own_sem.at[1])
    own_lags.start()
    per_peer(
        me,
        lambda peer: send(
            lag_rows.at[peer], lags_out.at[me], send_sem.at[1], lag_sem, {"seq": peer}
        ),
    )

    def await_bytes(part, *semaphores):
        for semaphore in semaphores:
            pltpu.make_async_copy(part, part, semaphore).wait()

    ends = [16 * at_y + 2 * z + at_core for at_y in around_y for at_core in (1 - core, core)]
    column = [16 * y + 2 * at_z + at_core for at_z in around_z for at_core in (1 - core, core)]
    real_line = readout_all.at[0, :, z, core]
    imag_line = readout_all.at[1, y, :, core]
    seven = readout_all.at[0, pl.ds(0, 7), 0, 0]
    await_bytes(seven, readout_sem.at[0])
    for peer in column[:-1]:
        send(real_line, real_line, send_sem.at[7], readout_sem.at[2], {"seq": peer})
    await_bytes(seven, readout_sem.at[1])
    for peer in ends[:-1]:
        send(imag_line, imag_line, send_sem.at[8], readout_sem.at[3], {"seq": peer})

    most = state_in.reshape(32, 1, WIDTH).at[pl.ds(0, 31)]
    await_bytes(most, state_sem)
    await_bytes(step_in.at[pl.ds(0, 7)], step_sem)
    column_rows[0:2, :] = sum_in_order(step_in, 8)
    column_rows[2:3, :] = sum_rows(state_in.reshape(32, WIDTH)[...])
    column_rows[3:4, :] = jnp.zeros_like(step_row)
    column_in[2 * z + core] = column_rows[...]
    for peer in column[:-1]:
        send(column_rows, column_in.at[2 * z + core], send_sem.at[5], column_sem, {"seq": peer})

    fifteen = readout_all.at[0].reshape(16, 8, 1, WIDTH).at[pl.ds(0, 15)]
    await_bytes(fifteen, readout_sem.at[2], readout_sem.at[3])
    sorted_ = sort_channels(readout_all.reshape(2, OWNERS, WIDTH))
    sorted_out[0] = sorted_[:STATES]
    sorted_out[1] = sorted_[STATES:]
    own_lags.wait()
    part = lags_out.at[pl.ds(0, OWNERS - 1)]
    await_bytes(part, lag_sem, send_sem.at[1])
    await_bytes(fifteen, send_sem.at[7], send_sem.at[8])
    await_bytes(seven, send_sem.at[2], send_sem.at[6])
    await_bytes(rest, send_sem.at[0])
    await_bytes(most, send_sem.at[3])
    await_bytes(step_in.at[pl.ds(0, 7)], send_sem.at[4])
    ended = column_in.at[pl.ds(0, 15)]
    await_bytes(ended, column_sem)
    sums = sum_in_order(column_in, 16)
    step_out[...] = sums[0:2, :]
    state_out[0:1, :] = sums[2:3, :STATES]
    state_out[1:2, :] = sums[2:3, STATES:]
    await_bytes(ended, send_sem.at[5])


def sum_in_order(buffer, count):
    parts = [buffer[place] for place in range(count)]
    while len(parts) > 1:
        parts = [parts[place] + parts[place + 1] for place in range(0, len(parts), 2)]
    return parts[0]


def sort_channels(rows_ref):
    blocks = []
    for part in range(2):
        turned = jnp.transpose(rows_ref[part], (1, 0))
        blocks.append(jnp.concatenate([turned[:STATES], turned[STATES:]], axis=1))
    value = jnp.concatenate(blocks, axis=0)
    at_row = lax.broadcasted_iota(jnp.int32, (2 * OWNERS, 2 * OWNERS), 0)
    at_column = lax.broadcasted_iota(jnp.int32, (2 * OWNERS, 2 * OWNERS), 1)
    places = jnp.where(at_row < OWNERS, 2 * at_row, 2 * at_row - 2 * OWNERS + 1)
    order = jnp.where(at_column == places, 1.0, 0.0).astype(jnp.bfloat16)
    high = value.astype(jnp.bfloat16)
    middle, low = halves(value - high.astype(jnp.float32))
    return dot(high, order) + (dot(middle, order) + dot(low, order))


def finish(*refs):
    count = len(refs) // 2
    copies = [
        pltpu.make_async_copy(refs[place], refs[count + place], refs[-1].at[place])
        for place in range(count)
    ]
    for copy in copies:
        copy.start()
    for copy in copies:
        copy.wait()


def keep(value):
    return pltpu.with_memory_space_constraint(value, pltpu.VMEM)


def per_device(tables, inputs, out_grad, readout, log_step, decay_log, rotation):
    norm_scale = 1.0 / math.sqrt(LENGTH)
    dma = pltpu.SemaphoreType.DMA
    any_space = pl.BlockSpec(memory_space=pl.ANY)
    vmem = pl.BlockSpec(memory_space=pltpu.VMEM)
    f32 = jnp.float32
    results = pl.pallas_call(
        functools.partial(kernel, norm_scale),
        out_shape=(
            pltpu.VMEM((OWNERS, 2, WIDTH), f32),
            pltpu.VMEM((2, STATES, 2 * OWNERS), f32),
            pltpu.VMEM((2, WIDTH), f32),
            pltpu.VMEM((2, STATES), f32),
        ),
        in_specs=[any_space] * 11,
        out_specs=(vmem,) * 4,
        scratch_shapes=[
            pltpu.VMEM((2, OWNERS, 2, WIDTH), jnp.bfloat16),
            pltpu.VMEM((2, OWNERS, 2, WIDTH), jnp.bfloat16),
            pltpu.VMEM((OWNERS, 2, WIDTH), f32),
            pltpu.VMEM((2, 1, WIDTH), f32),
            pltpu.VMEM((2, 8, 8, 2, 1, WIDTH), f32),
            pltpu.VMEM((2 * OWNERS, WIDTH), f32),
            pltpu.VMEM((1, WIDTH), f32),
            pltpu.VMEM((4, 8, 1, WIDTH), f32),
            pltpu.VMEM((2, WIDTH), f32),
            pltpu.VMEM((8, 2, WIDTH), f32),
            pltpu.VMEM((4, WIDTH), f32),
            pltpu.VMEM((16, 4, WIDTH), f32),
        ]
        + [
            pltpu.VMEM((2, STATES, 2 * OWNERS), f32),
            pltpu.SMEM((2 * OWNERS,), f32),
            pltpu.VMEM((1, STATES), f32),
            pltpu.VMEM((1, STATES), f32),
        ]
        + [pltpu.VMEM(table.shape, table.dtype) for table in tables]
        + [dma((2,)), dma((9,)), dma((2,)), dma((9,)), dma, dma, dma((4,)), dma, dma, dma],
        compiler_params=pltpu.CompilerParams(collective_id=0, has_side_effects=True),
        name="channel_rows",
    )(
        inputs.reshape(OWNERS, 2, WIDTH),
        out_grad.reshape(OWNERS, 2, WIDTH),
        jnp.transpose(readout, (0, 2, 1)),
        log_step,
        decay_log.reshape(1, STATES),
        rotation.reshape(1, STATES),
        *[jnp.asarray(table) for table in tables],
    )
    kernel_grad, readout_grad, step_grad, state_grad = pl.pallas_call(
        finish,
        out_shape=(
            jax.ShapeDtypeStruct((2 * OWNERS, WIDTH), f32),
            jax.ShapeDtypeStruct((2, STATES, 2 * OWNERS), f32),
            jax.ShapeDtypeStruct((2, WIDTH), f32),
            jax.ShapeDtypeStruct((2, STATES), f32),
        ),
        in_specs=[vmem] * 4,
        out_specs=(any_space,) * 4,
        scratch_shapes=[dma((4,))],
        name="finish",
    )(*[keep(value) for value in (results[0].reshape(2 * OWNERS, WIDTH), *results[1:])])
    return (
        kernel_grad,
        jnp.transpose(readout_grad, (0, 2, 1)),
        step_grad.reshape(2 * OWNERS),
        state_grad,
    )


def solution(mesh):
    tables = transform_tables()
    return jax.shard_map(
        functools.partial(per_device, tables),
        mesh=mesh,
        in_specs=(P("ch", "seq"), P("ch", "seq"), P(None, "ch", None), P("ch"), P(), P()),
        out_specs=(P("ch", "seq"), P(None, "ch", None), P("ch"), P()),
        check_vma=False,
    )
```

```python
import functools
import math

import jax
import jax.numpy as jnp
import numpy as np
from jax import lax
from jax.experimental import pallas as pl
from jax.experimental.pallas import tpu as pltpu
from jax.sharding import PartitionSpec as P

MESH = pl.DeviceIdType.MESH
OWNERS = 128
WIDTH = 128
LENGTH = OWNERS * WIDTH
STATES = 64


def split_table(table):
    high = np.asarray(table, np.float32).astype(jnp.bfloat16)
    low = (np.asarray(table, np.float64) - high.astype(np.float64)).astype(jnp.bfloat16)
    return np.stack([high, low])


def transform_tables():
    index = np.arange(WIDTH, dtype=np.float64)
    quarter = index + 0.25
    enter = 2.0 * np.pi * np.outer(quarter, index) / WIDTH
    spread = np.zeros((2, 2, WIDTH, OWNERS, 2))
    for channel in range(2):
        spread[0, channel, :, :, channel] = np.cos(enter)
        spread[1, channel, :, :, channel] = -np.sin(enter)
    first = spread.reshape(4 * WIDTH, 2 * OWNERS)
    turn = 2.0 * np.pi * np.outer(quarter, index) / LENGTH
    turns = np.stack([np.cos(turn), np.sin(turn)]).astype(np.float32)
    plain = 2.0 * np.pi * np.outer(index, index) / WIDTH
    cosine, sine = np.cos(plain), np.sin(plain)
    second = np.block([[cosine, -sine], [sine, cosine]])
    third = np.block([[cosine, sine], [-sine, cosine]])
    scale = 1.0 / (LENGTH * math.sqrt(LENGTH))
    leave = enter.T
    fourth = np.concatenate([np.cos(leave), -np.sin(leave)], axis=1) * scale
    return (
        split_table(first),
        turns,
        split_table(second),
        split_table(third),
        split_table(fourth),
    )


def dot(left, right):
    return jnp.dot(left, right, preferred_element_type=jnp.float32)


def halves(value):
    high = value.astype(jnp.bfloat16)
    return high, (value - high.astype(jnp.float32)).astype(jnp.bfloat16)


def dot_pair(left, right):
    return dot(left[0], right[0]) + (dot(left[0], right[1]) + dot(left[1], right[0]))


def sine_cosine(angle):
    turns = jnp.floor(angle * (2.0 / math.pi) + 0.5)
    rest = angle - turns * 1.5625
    rest = rest - turns * 0.0081787109375
    rest = rest - turns * 0.000116348266601562
    rest = rest - turns * 1.26759079665e-06
    square = rest * rest
    sine = rest + rest * square * (
        -1.6666667e-1 + square * (8.3333310e-3 + square * (-1.9840874e-4 + square * 2.7525562e-6))
    )
    cosine = (
        1.0
        - 0.5 * square
        + square
        * square
        * (4.16666667e-2 + square * (-1.38888889e-3 + square * (2.48015873e-5 - square * 2.7557319e-7)))
    )
    quadrant = turns - 4.0 * jnp.floor(turns * 0.25)
    odd = (quadrant == 1.0) | (quadrant == 3.0)
    sine_out = jnp.where(odd, cosine, sine)
    cosine_out = jnp.where(odd, sine, cosine)
    sine_out = jnp.where(quadrant >= 2.0, -sine_out, sine_out)
    cosine_out = jnp.where((quadrant == 1.0) | (quadrant == 2.0), -cosine_out, cosine_out)
    return sine_out, cosine_out


def exp_minus_one(value):
    series = 1.0 + value * (1.0 / 9.0)
    for count in (8.0, 7.0, 6.0, 5.0, 4.0, 3.0, 2.0):
        series = 1.0 + value * (1.0 / count) * series
    return jnp.where(jnp.abs(value) < 0.5, value * series, jnp.exp(value) - 1.0)


def multiply(left, right):
    return (left[0] * right[0] - left[1] * right[1], left[0] * right[1] + left[1] * right[0])


def conjugate(value):
    return (value[0], -value[1])


def primal_rows(step, decay, turn, readout):
    pole = (-jnp.exp(decay), turn)
    rate = (step * pole[0], step * pole[1])
    sine, cosine = sine_cosine(rate[1])
    half_sine, _ = sine_cosine(0.5 * rate[1])
    growth = jnp.exp(rate[0])
    lift = (
        exp_minus_one(rate[0]) * cosine - 2.0 * half_sine * half_sine,
        growth * sine,
    )
    norm = pole[0] * pole[0] + pole[1] * pole[1]
    inverse = (pole[0] / norm, -pole[1] / norm)
    ratio = multiply(lift, inverse)
    coef = multiply(readout, ratio)
    power = (growth * cosine, growth * sine)
    return dict(
        step=step, pole=pole, rate=rate, inverse=inverse, ratio=ratio, coef=coef, power=power
    )


def power_table(rate, positions):
    decays = jnp.exp(rate[0] * positions)
    sine, cosine = sine_cosine(rate[1] * positions)
    return decays * cosine, decays * sine


def correlate(signals, first, turns, second, third, fourth):
    spread = dot(first[0], signals) + dot(first[1], signals)
    turn_cos, turn_sin = turns[0], turns[1]
    blocks = []
    for channel in range(2):
        for signal in range(2):
            columns = slice(signal * WIDTH, (signal + 1) * WIDTH)
            real = spread[channel * WIDTH : (channel + 1) * WIDTH, columns]
            imag = spread[(2 + channel) * WIDTH : (3 + channel) * WIDTH, columns]
            blocks.append(
                jnp.concatenate(
                    [real * turn_cos + imag * turn_sin, imag * turn_cos - real * turn_sin], axis=1
                )
            )
    spectrum = dot_pair(halves(jnp.concatenate(blocks, axis=0)), second)
    products = []
    for channel in range(2):
        entry = spectrum[2 * channel * WIDTH : (2 * channel + 1) * WIDTH]
        exit_ = spectrum[(2 * channel + 1) * WIDTH : (2 * channel + 2) * WIDTH]
        in_real, in_imag = entry[:, :WIDTH], entry[:, WIDTH:]
        out_real, out_imag = exit_[:, :WIDTH], exit_[:, WIDTH:]
        products.append(
            jnp.concatenate(
                [
                    out_real * in_real + out_imag * in_imag,
                    out_imag * in_real - out_real * in_imag,
                ],
                axis=1,
            )
        )
    back = dot_pair(halves(jnp.concatenate(products, axis=0)), third)
    columns = []
    for channel in range(2):
        real = back[channel * WIDTH : (channel + 1) * WIDTH, :WIDTH]
        imag = back[channel * WIDTH : (channel + 1) * WIDTH, WIDTH:]
        columns.append(
            jnp.concatenate(
                [real * turn_cos - imag * turn_sin, real * turn_sin + imag * turn_cos], axis=0
            )
        )
    return dot_pair((fourth[0], fourth[1]), halves(jnp.concatenate(columns, axis=1)))


def sum_rows(value):
    return jnp.sum(value, axis=0, keepdims=True)


def power_sums(lags, tables, base, starts, norm_scale):
    stacked = jnp.concatenate([lags[:, :WIDTH], lags[:, WIDTH:]], axis=0)
    raw = dot_pair(halves(stacked), tables)
    lane = lax.broadcasted_iota(jnp.int32, (OWNERS, WIDTH), 1)
    picked = [
        jnp.where(
            lane < STATES,
            raw[:OWNERS, part * WIDTH : (part + 1) * WIDTH],
            raw[OWNERS:, part * WIDTH : (part + 1) * WIDTH],
        )
        for part in range(4)
    ]
    plain = (picked[0], picked[1])
    lagged = (starts * picked[0] + picked[2], starts * picked[1] + picked[3])
    powers = multiply(base, plain)
    lag_powers = multiply(base, lagged)
    return (
        (norm_scale * sum_rows(powers[0]), norm_scale * sum_rows(powers[1])),
        (norm_scale * sum_rows(lag_powers[0]), norm_scale * sum_rows(lag_powers[1])),
    )


def parameter_rows(primal, readout, powers, lag_powers):
    coef_grad = (2.0 * powers[0], -2.0 * powers[1])
    readout_grad = multiply(conjugate(primal["ratio"]), coef_grad)
    ratio_grad = multiply(conjugate(readout), coef_grad)
    shifted = multiply(primal["coef"], lag_powers)
    lift_grad = multiply(conjugate(primal["inverse"]), ratio_grad)
    through = multiply(conjugate(primal["power"]), lift_grad)
    rate_grad = (2.0 * shifted[0] + through[0], -2.0 * shifted[1] + through[1])
    direct = multiply(conjugate(primal["ratio"]), lift_grad)
    step, pole = primal["step"], primal["pole"]
    pole_grad = (step * rate_grad[0] - direct[0], step * rate_grad[1] - direct[1])
    step_terms = step * (rate_grad[0] * pole[0] + rate_grad[1] * pole[1])
    return readout_grad, step_terms, (pole_grad[0] * pole[0], pole_grad[1])


def offset_of(place, ring):
    return ring // 2 + (1 - 2 * (place % 2)) * ((place + 1) // 2)


def place_of(me):
    return me // 16, (me // 2) % 8, me % 2


def ring_places(place, ring):
    return [(place + offset_of(count, ring)) % ring for count in range(ring)]


def hop_order():
    draws = np.random.RandomState(0).permutation(OWNERS)
    offsets = [(at // 16, at // 2 % 8, at % 2) for at in range(1, OWNERS)]
    hops = [min(y, 8 - y) + min(z, 8 - z) for y, z, _ in offsets]
    places = sorted(range(OWNERS - 1), key=lambda at: (-hops[at], draws[at]))
    return [offsets[at] for at in places]


def per_peer(me, action):
    y, z, core = place_of(me)
    to_y = [16 * ((y + step) % 8) for step in range(8)]
    to_z = [2 * ((z + step) % 8) for step in range(8)]
    to_core = [core, 1 - core]
    for step_y, step_z, step_core in hop_order():
        action(to_y[step_y] + to_z[step_z] + to_core[step_core])


def kernel(
    norm_scale,
    inputs_ref,
    grads_ref,
    readout_in,
    log_step_in,
    decay_in,
    rotation_in,
    first_ref,
    turns_ref,
    second_ref,
    third_ref,
    fourth_ref,
    lags_out,
    sorted_out,
    step_out,
    state_out,
    outgoing,
    arrived,
    lag_rows,
    readout_rows,
    readout_all,
    readout_turned,
    state_rows,
    state_in,
    step_rows,
    step_in,
    column_rows,
    column_in,
    order,
    readout_ref,
    log_step_ref,
    decay_ref,
    rotation_ref,
    first,
    turns,
    second,
    third,
    fourth,
    stage_sem,
    table_sem,
    own_sem,
    send_sem,
    signal_sem,
    lag_sem,
    readout_sem,
    state_sem,
    step_sem,
    column_sem,
):
    me = lax.axis_index("seq")
    row = lax.axis_index("ch")
    y, z, core = place_of(me)
    stages = [
        pltpu.make_async_copy(inputs_ref, outgoing.at[0], stage_sem.at[0]),
        pltpu.make_async_copy(grads_ref, outgoing.at[1], stage_sem.at[1]),
    ]
    for copy in stages:
        copy.start()
    barrier = pltpu.get_barrier_semaphore()

    def greet(peer):
        pl.semaphore_signal(barrier, inc=1, device_id={"seq": peer}, device_id_type=MESH)

    per_peer(me, greet)
    around_y = ring_places(y, 8)
    around_z = ring_places(z, 8)
    around_x = [(row + step) % 4 for step in (2, 1, 3, 0)]
    across = [(at_x, 16 * at_y + 2 * z + core) for at_x in around_x[:3] for at_y in around_y]
    for at_x, peer in across:
        pl.semaphore_signal(
            barrier, inc=1, device_id={"ch": at_x, "seq": peer}, device_id_type=MESH
        )
    loads = [
        pltpu.make_async_copy(source, target, table_sem.at[place])
        for place, (source, target) in enumerate(
            (
                (log_step_in, log_step_ref),
                (decay_in, decay_ref),
                (rotation_in, rotation_ref),
                (readout_in, readout_ref),
                (first_ref, first),
                (turns_ref, turns),
                (second_ref, second),
                (third_ref, third),
                (fourth_ref, fourth),
            )
        )
    ]
    for copy in loads:
        copy.start()
    for copy in stages:
        copy.wait()
    pl.semaphore_wait(barrier, OWNERS - 1 + len(across))

    def send(source, target, sent, received, device):
        pltpu.make_async_remote_copy(
            src_ref=source,
            dst_ref=target,
            send_sem=sent,
            recv_sem=received,
            device_id=device,
            device_id_type=MESH,
        ).start()

    own = pltpu.make_async_copy(outgoing.at[:, me], arrived.at[:, me], own_sem.at[0])
    own.start()
    per_peer(
        me,
        lambda peer: send(
            outgoing.at[:, peer], arrived.at[:, me], send_sem.at[0], signal_sem, {"seq": peer}
        ),
    )

    for copy in loads[:4]:
        copy.wait()
    lane_row = lax.broadcasted_iota(jnp.int32, (1, WIDTH), 1)
    left = lane_row < STATES
    step_row = jnp.exp(jnp.where(left, log_step_ref[2 * me], log_step_ref[2 * me + 1]))
    decay_row = jnp.concatenate([decay_ref[...], decay_ref[...]], axis=1)
    turn_row = jnp.concatenate([rotation_ref[...], rotation_ref[...]], axis=1)
    readout_turned[...] = jnp.transpose(
        jnp.concatenate([readout_ref[0], readout_ref[1]], axis=0), (1, 0)
    )
    low = readout_turned[pl.ds(2 * me, 1), :]
    high = readout_turned[pl.ds(2 * me + 1, 1), :]
    readout = (
        jnp.where(left, low, pltpu.roll(high, STATES, 1)),
        jnp.where(left, pltpu.roll(low, STATES, 1), high),
    )
    primal = primal_rows(step_row, decay_row, turn_row, readout)
    offsets = lax.broadcasted_iota(jnp.int32, (WIDTH, WIDTH), 0).astype(jnp.float32)
    starts = offsets * float(WIDTH)
    near = power_table(primal["rate"], offsets)
    base = power_table(primal["rate"], starts)
    tables = halves(
        jnp.concatenate([near[0], near[1], offsets * near[0], offsets * near[1]], axis=1)
    )
    for copy in loads[4:]:
        copy.wait()

    order[...] = channel_order()
    own.wait()
    rest = arrived.at[:, pl.ds(0, OWNERS - 1)]
    pltpu.make_async_copy(rest, rest, signal_sem).wait()
    signals = jnp.concatenate(
        [arrived.reshape(2, 2 * OWNERS, WIDTH)[0], arrived.reshape(2, 2 * OWNERS, WIDTH)[1]],
        axis=1,
    )
    lags = correlate(signals, first, turns, second, third, fourth)
    lag_rows[:, 0, :] = lags[:, :WIDTH]
    lag_rows[:, 1, :] = lags[:, WIDTH:]

    powers, lag_powers = power_sums(lags, tables, base, starts, norm_scale)
    readout_grad, step_terms, state_grad = parameter_rows(primal, readout, powers, lag_powers)
    state_rows[...] = jnp.where(
        left,
        state_grad[0] + pltpu.roll(state_grad[0], STATES, 1),
        state_grad[1] + pltpu.roll(state_grad[1], STATES, 1),
    )
    line = [16 * at_y + 2 * z + core for at_y in around_y[:-1]]
    for at_x, peer in across + [(around_x[3], peer) for peer in line]:
        send(
            state_rows,
            state_in.at[row, y],
            send_sem.at[3],
            state_sem,
            {"ch": at_x, "seq": peer},
        )
    state_in[row, y] = state_rows[...]
    first_step = jnp.sum(jnp.where(left, step_terms, 0.0), axis=1, keepdims=True)
    second_step = jnp.sum(jnp.where(left, 0.0, step_terms), axis=1, keepdims=True)
    count = WIDTH * lax.broadcasted_iota(jnp.int32, (2, WIDTH), 0) + lax.broadcasted_iota(
        jnp.int32, (2, WIDTH), 1
    )
    step_rows[...] = jnp.where(
        count == 2 * me, first_step, jnp.where(count == 2 * me + 1, second_step, 0.0)
    )
    step_in[y] = step_rows[...]
    readout_rows[0] = readout_grad[0]
    readout_rows[1] = readout_grad[1]
    readout_all[0, y, z, core] = readout_grad[0]
    readout_all[1, y, z, core] = readout_grad[1]
    for peer in line:
        send(
            readout_rows.at[0],
            readout_all.at[0, y, z, core],
            send_sem.at[2],
            readout_sem.at[0],
            {"seq": peer},
        )
    for at_z in around_z[:-1]:
        send(
            readout_rows.at[1],
            readout_all.at[1, y, z, core],
            send_sem.at[6],
            readout_sem.at[1],
            {"seq": 16 * y + 2 * at_z + core},
        )
    for peer in line:
        send(step_rows, step_in.at[y], send_sem.at[4], step_sem, {"seq": peer})
    own_lags = pltpu.make_async_copy(lag_rows.at[me], lags_out.at[me], own_sem.at[1])
    own_lags.start()
    per_peer(
        me,
        lambda peer: send(
            lag_rows.at[peer], lags_out.at[me], send_sem.at[1], lag_sem, {"seq": peer}
        ),
    )

    def await_bytes(part, *semaphores):
        for semaphore in semaphores:
            pltpu.make_async_copy(part, part, semaphore).wait()

    ends = [16 * at_y + 2 * z + at_core for at_y in around_y for at_core in (1 - core, core)]
    column = [16 * y + 2 * at_z + at_core for at_z in around_z for at_core in (1 - core, core)]
    real_line = readout_all.at[0, :, z, core]
    imag_line = readout_all.at[1, y, :, core]
    seven = readout_all.at[0, pl.ds(0, 7), 0, 0]
    await_bytes(seven, readout_sem.at[0])
    for peer in column[:-1]:
        send(real_line, real_line, send_sem.at[7], readout_sem.at[2], {"seq": peer})
    await_bytes(seven, readout_sem.at[1])
    for peer in ends[:-1]:
        send(imag_line, imag_line, send_sem.at[8], readout_sem.at[3], {"seq": peer})

    most = state_in.reshape(32, 1, WIDTH).at[pl.ds(0, 31)]
    await_bytes(most, state_sem)
    await_bytes(step_in.at[pl.ds(0, 7)], step_sem)
    column_rows[0:2, :] = sum_in_order(step_in, 8)
    column_rows[2:3, :] = sum_rows(state_in.reshape(32, WIDTH)[...])
    column_rows[3:4, :] = jnp.zeros_like(step_row)
    column_in[2 * z + core] = column_rows[...]
    for peer in column[:-1]:
        send(column_rows, column_in.at[2 * z + core], send_sem.at[5], column_sem, {"seq": peer})

    fifteen = readout_all.at[0].reshape(16, 8, 1, WIDTH).at[pl.ds(0, 15)]
    rows = readout_all.reshape(2, OWNERS, WIDTH)
    for part in range(2):
        await_bytes(fifteen, readout_sem.at[2 + part])
        sorted_out[part] = sort_channels(rows[part], order[...])
    own_lags.wait()
    part = lags_out.at[pl.ds(0, OWNERS - 1)]
    await_bytes(part, lag_sem, send_sem.at[1])
    await_bytes(fifteen, send_sem.at[7], send_sem.at[8])
    await_bytes(seven, send_sem.at[2], send_sem.at[6])
    await_bytes(rest, send_sem.at[0])
    await_bytes(most, send_sem.at[3])
    await_bytes(step_in.at[pl.ds(0, 7)], send_sem.at[4])
    ended = column_in.at[pl.ds(0, 15)]
    await_bytes(ended, column_sem)
    sums = sum_in_order(column_in, 16)
    step_out[...] = sums[0:2, :]
    state_out[0:1, :] = sums[2:3, :STATES]
    state_out[1:2, :] = sums[2:3, STATES:]
    await_bytes(ended, send_sem.at[5])


def sum_in_order(buffer, count):
    parts = [buffer[place] for place in range(count)]
    while len(parts) > 1:
        parts = [parts[place] + parts[place + 1] for place in range(0, len(parts), 2)]
    return parts[0]


def channel_order():
    at_row = lax.broadcasted_iota(jnp.int32, (2 * OWNERS, 2 * OWNERS), 0)
    at_column = lax.broadcasted_iota(jnp.int32, (2 * OWNERS, 2 * OWNERS), 1)
    places = jnp.where(at_row < OWNERS, 2 * at_row, 2 * at_row - 2 * OWNERS + 1)
    return jnp.where(at_column == places, 1.0, 0.0).astype(jnp.bfloat16)


def sort_channels(rows, order):
    turned = jnp.transpose(rows, (1, 0))
    value = jnp.concatenate([turned[:STATES], turned[STATES:]], axis=1)
    high = value.astype(jnp.bfloat16)
    middle, low = halves(value - high.astype(jnp.float32))
    return dot(high, order) + (dot(middle, order) + dot(low, order))


def finish(*refs):
    count = len(refs) // 2
    copies = [
        pltpu.make_async_copy(refs[place], refs[count + place], refs[-1].at[place])
        for place in range(count)
    ]
    for copy in copies:
        copy.start()
    for copy in copies:
        copy.wait()


def keep(value):
    return pltpu.with_memory_space_constraint(value, pltpu.VMEM)


def per_device(tables, inputs, out_grad, readout, log_step, decay_log, rotation):
    norm_scale = 1.0 / math.sqrt(LENGTH)
    dma = pltpu.SemaphoreType.DMA
    any_space = pl.BlockSpec(memory_space=pl.ANY)
    vmem = pl.BlockSpec(memory_space=pltpu.VMEM)
    f32 = jnp.float32
    results = pl.pallas_call(
        functools.partial(kernel, norm_scale),
        out_shape=(
            pltpu.VMEM((OWNERS, 2, WIDTH), f32),
            pltpu.VMEM((2, STATES, 2 * OWNERS), f32),
            pltpu.VMEM((2, WIDTH), f32),
            pltpu.VMEM((2, STATES), f32),
        ),
        in_specs=[any_space] * 11,
        out_specs=(vmem,) * 4,
        scratch_shapes=[
            pltpu.VMEM((2, OWNERS, 2, WIDTH), jnp.bfloat16),
            pltpu.VMEM((2, OWNERS, 2, WIDTH), jnp.bfloat16),
            pltpu.VMEM((OWNERS, 2, WIDTH), f32),
            pltpu.VMEM((2, 1, WIDTH), f32),
            pltpu.VMEM((2, 8, 8, 2, 1, WIDTH), f32),
            pltpu.VMEM((2 * OWNERS, WIDTH), f32),
            pltpu.VMEM((1, WIDTH), f32),
            pltpu.VMEM((4, 8, 1, WIDTH), f32),
            pltpu.VMEM((2, WIDTH), f32),
            pltpu.VMEM((8, 2, WIDTH), f32),
            pltpu.VMEM((4, WIDTH), f32),
            pltpu.VMEM((16, 4, WIDTH), f32),
            pltpu.VMEM((2 * OWNERS, 2 * OWNERS), jnp.bfloat16),
        ]
        + [
            pltpu.VMEM((2, STATES, 2 * OWNERS), f32),
            pltpu.SMEM((2 * OWNERS,), f32),
            pltpu.VMEM((1, STATES), f32),
            pltpu.VMEM((1, STATES), f32),
        ]
        + [pltpu.VMEM(table.shape, table.dtype) for table in tables]
        + [dma((2,)), dma((9,)), dma((2,)), dma((9,)), dma, dma, dma((4,)), dma, dma, dma],
        compiler_params=pltpu.CompilerParams(collective_id=0, has_side_effects=True),
        name="channel_rows",
    )(
        inputs.reshape(OWNERS, 2, WIDTH),
        out_grad.reshape(OWNERS, 2, WIDTH),
        jnp.transpose(readout, (0, 2, 1)),
        log_step,
        decay_log.reshape(1, STATES),
        rotation.reshape(1, STATES),
        *[jnp.asarray(table) for table in tables],
    )
    kernel_grad, readout_grad, step_grad, state_grad = pl.pallas_call(
        finish,
        out_shape=(
            jax.ShapeDtypeStruct((2 * OWNERS, WIDTH), f32),
            jax.ShapeDtypeStruct((2, STATES, 2 * OWNERS), f32),
            jax.ShapeDtypeStruct((2, WIDTH), f32),
            jax.ShapeDtypeStruct((2, STATES), f32),
        ),
        in_specs=[vmem] * 4,
        out_specs=(any_space,) * 4,
        scratch_shapes=[dma((4,))],
        name="finish",
    )(*[keep(value) for value in (results[0].reshape(2 * OWNERS, WIDTH), *results[1:])])
    return (
        kernel_grad,
        jnp.transpose(readout_grad, (0, 2, 1)),
        step_grad.reshape(2 * OWNERS),
        state_grad,
    )


def solution(mesh):
    tables = transform_tables()
    return jax.shard_map(
        functools.partial(per_device, tables),
        mesh=mesh,
        in_specs=(P("ch", "seq"), P("ch", "seq"), P(None, "ch", None), P("ch"), P(), P()),
        out_specs=(P("ch", "seq"), P(None, "ch", None), P("ch"), P()),
        check_vma=False,
    )
```
